128 devices in a mesh: gy: 32 (over z_hi, x, y), gz: 4 (over z_lo, core).
Axes of the slice: x: 4, y: 4, z: 4 (z_hi: 2, z_lo: 2; z = z_hi * 2 + z_lo), core: 2. Of those that a mesh axis runs over, the one named last changes fastest.
Arguments:
- hessian_one: bfloat16 [6, 256, 256, 256], P(None, 'gy', 'gz'), may hold values from -1 to 1
- hessian_two: bfloat16 [6, 256, 256, 256], P(None, 'gy', 'gz'), may hold values from -0.796875 to 0.796875
- displacement: float32 [3, 256, 256, 256], P(None, 'gy', 'gz'), may hold values from -0.5 to 0.5
Outputs:
- psi_third: float32 [3, 256, 256, 256], P(None, 'gy', 'gz')
- overdensity: float32 [256, 256, 256], P('gy', 'gz')
The draws below stay inside these ranges and needn't reach their ends.
All inputs are finite; a program needn't handle non-finite values.
Results may differ from the reference program's by a relative error of at most 0.0003.
Values sent between devices are 32-bit elements; how exact they have to be, the bound alone decides.
No kernel may reach another device: no remote copies, remote signals or barrier semaphores. Data moves between devices by JAX's collectives and lax.ppermute only.
A program may use at most 128 MiB of HBM per device.

```python
import jax
import jax.numpy as jnp

NX = 256
NY = 256
NZ = 256


def block_levels(own_key, dims, cuts, least, high):
    factor_of = 1.0
    for dim, parts in cuts:
        steps = jax.random.uniform(jax.random.fold_in(jax.random.fold_in(own_key, 6), dim), (parts,), jnp.float32, least / len(cuts), high / len(cuts))
        factor_of = factor_of * jnp.repeat(jnp.exp(steps), dims[dim] // parts).reshape((-1,) + (1,) * (len(dims) - 1 - dim))
    return factor_of


def setup_inputs(seed: int = 0) -> dict:
    arg_keys = jax.random.split(jax.random.key(seed), 4)
    hessian_one = jnp.clip(jax.random.uniform(arg_keys[0], (6, NY, NZ, NX), jnp.float32, -1.0, 1.0) * block_levels(arg_keys[0], (6, NY, NZ, NX), ((1, 32), (2, 4)), -0.4, 0.0), -1.0, 1.0).astype(jnp.bfloat16)
    hessian_two = jnp.clip(jax.random.uniform(arg_keys[1], (6, NY, NZ, NX), jnp.float32, -0.796875, 0.796875) * block_levels(arg_keys[1], (6, NY, NZ, NX), ((1, 32), (2, 4)), -0.4, 0.0), -0.796875, 0.796875).astype(jnp.bfloat16)
    displacement = jnp.clip(jax.random.uniform(arg_keys[2], (3, NY, NZ, NX), jnp.float32, -0.5, 0.5) * block_levels(arg_keys[2], (3, NY, NZ, NX), ((1, 32), (2, 4)), -0.4, 0.0), -0.5, 0.5)
    return dict(hessian_one=hessian_one, hessian_two=hessian_two, displacement=displacement)


det_weight = -1.0 / 3.0
mixed_weight = 10.0 / 21.0


def spline(shifted):
    distance = jnp.abs(shifted)
    inside = 2.0 / 3.0 - distance * distance + 0.5 * distance * distance * distance
    outer_gap = jnp.maximum(2.0 - distance, 0.0)
    outside = outer_gap * outer_gap * outer_gap / 6.0
    return jnp.where(distance < 1.0, inside, outside)


def source_term(hessian_one, hessian_two):
    primary = [hessian_one[component].astype(jnp.float32) for component in range(6)]
    secondary = [hessian_two[component].astype(jnp.float32) for component in range(6)]
    determinant = (primary[0] * (primary[1] * primary[2] - primary[5] * primary[5])
                   - primary[3] * (primary[3] * primary[2] - primary[5] * primary[4])
                   + primary[4] * (primary[3] * primary[5] - primary[1] * primary[4]))
    mixed = 0.5 * (secondary[0] * (primary[1] + primary[2]) + secondary[1] * (primary[0] + primary[2])
                   + secondary[2] * (primary[0] + primary[1]))
    mixed = mixed - (secondary[3] * primary[3] + secondary[4] * primary[4] + secondary[5] * primary[5])
    return det_weight * determinant + mixed_weight * mixed


def wave_table(count):
    position = jnp.arange(count, dtype=jnp.int32)
    signed = jnp.where(position * 2 > count, position - count, position)
    return signed.astype(jnp.float32) * (2.0 * jnp.pi / count)


def slope_table(count):
    position = jnp.arange(count, dtype=jnp.int32)
    return jnp.where(position * 2 == count, 0.0, wave_table(count))


def reference(hessian_one, hessian_two, displacement):
    source = source_term(hessian_one, hessian_two)
    spectrum = jnp.fft.fftn(source)
    wave_rows = wave_table(NY)[:, None, None]
    wave_depth = wave_table(NZ)[None, :, None]
    wave_lines = wave_table(NX)[None, None, :]
    squared = wave_rows * wave_rows + wave_depth * wave_depth + wave_lines * wave_lines
    safe_square = jnp.where(squared > 0.0, squared, 1.0)
    inverse = jnp.where(squared > 0.0, 1.0 / safe_square, 0.0)
    slopes = [slope_table(NX)[None, None, :], slope_table(NY)[:, None, None], slope_table(NZ)[None, :, None]]
    fields = []
    for slope_grid in slopes:
        rotated = 1j * (slope_grid * inverse) * spectrum
        fields.append(jnp.real(jnp.fft.ifftn(rotated)).astype(jnp.float32))
    psi_third = jnp.stack(fields)
    moved_by = displacement + psi_third
    line_weights = [spline(shift_line - 2.0 + moved_by[0]) for shift_line in range(5)]
    density = jnp.zeros(source.shape, jnp.float32)
    for shift_row in range(5):
        for shift_depth in range(5):
            plane_weight = spline(shift_row - 2.0 + moved_by[1]) * spline(shift_depth - 2.0 + moved_by[2])
            line_sum = jnp.zeros(source.shape, jnp.float32)
            for shift_line in range(5):
                line_sum = line_sum + jnp.roll(line_weights[shift_line] * plane_weight, 2 - shift_line, axis=2)
            density = density + jnp.roll(line_sum, (2 - shift_row, 2 - shift_depth), axis=(0, 1))
    return psi_third, density - 1.0
```

```python
import functools

import jax
import jax.numpy as jnp
import numpy as np
from jax import lax
from jax.experimental import pallas as pl
from jax.experimental.pallas import tpu as pltpu
from jax.sharding import PartitionSpec as P

N = 256
HALF = N // 2
ROWS = 8
DEPTH = 64
det_weight = -1.0 / 3.0
mixed_weight = 10.0 / 21.0
f32 = jnp.float32
bf16 = jnp.bfloat16


def split_table(table):
    high = table.astype(np.float32).astype(jnp.bfloat16)
    low = (table - high.astype(np.float64)).astype(np.float32).astype(jnp.bfloat16)
    return np.stack([high, low])


def wave_index():
    order = np.arange(N)
    return np.where(order <= HALF, order, order - HALF)


def real_tables():
    order = np.arange(N)
    wave = wave_index()
    is_sin = order > HALF
    angle = 2.0 * np.pi / N * (wave[:, None] * np.arange(N)[None, :] % N)
    cosine, sine = np.cos(angle), np.sin(angle)
    forward = np.where(is_sin[:, None], sine, cosine)
    single = (order == 0) | (order == HALF)
    weight = np.where(single, 1.0, 2.0)[:, None] / N
    inverse = weight * forward
    number = (2.0 * np.pi / N * np.where(single, 0, wave))[:, None]
    slope = weight * number * np.where(is_sin[:, None], cosine, -sine)
    return forward, inverse, slope


forward_table, inverse_table, slope_table = real_tables()


def split(value):
    high = value.astype(bf16)
    return high, (value - high.astype(f32)).astype(bf16)


def dot3(left, right, dims):
    (left_high, left_low), (right_high, right_low) = left, right
    product = functools.partial(
        lax.dot_general, dimension_numbers=(dims, ((), ())), preferred_element_type=f32
    )
    return product(left_high, right_high) + (
        product(left_high, right_low) + product(left_low, right_high)
    )


NN = ((1,), (0,))
NT = ((1,), (1,))
TN = ((0,), (0,))


def low_lanes(shape):
    return lax.broadcasted_iota(jnp.int32, shape, len(shape) - 1) < DEPTH


def source_term(one, two):
    primary = [one[c].astype(f32) for c in range(6)]
    secondary = [two[c].astype(f32) for c in range(6)]
    determinant = (
        primary[0] * (primary[1] * primary[2] - primary[5] * primary[5])
        - primary[3] * (primary[3] * primary[2] - primary[5] * primary[4])
        + primary[4] * (primary[3] * primary[5] - primary[1] * primary[4])
    )
    mixed = 0.5 * (
        secondary[0] * (primary[1] + primary[2])
        + secondary[1] * (primary[0] + primary[2])
        + secondary[2] * (primary[0] + primary[1])
    )
    mixed = mixed - (
        secondary[3] * primary[3] + secondary[4] * primary[4] + secondary[5] * primary[5]
    )
    return det_weight * determinant + mixed_weight * mixed


def lines_kernel(one_ref, two_ref, table_ref, out_ref):
    pair = pl.program_id(0)
    source = jnp.concatenate(
        [
            source_term(
                [one_ref[c, row] for c in range(6)], [two_ref[c, row] for c in range(6)]
            )
            for row in range(2)
        ],
        axis=0,
    )
    result = dot3((table_ref[0], table_ref[1]), split(source), NT)
    first, second = result[:HALF], result[HALF:]
    mask = low_lanes((HALF, 128))
    out_ref[pl.ds(2 * pair, HALF, stride=ROWS), :] = jnp.where(
        mask, first, pltpu.roll(second, DEPTH, 1)
    )
    out_ref[pl.ds(2 * pair + 1, HALF, stride=ROWS), :] = jnp.where(
        mask, pltpu.roll(first, DEPTH, 1), second
    )


def lines(one, two):
    spec = pl.BlockSpec((6, 2, DEPTH, N), lambda i: (0, i, 0, 0))
    return pl.pallas_call(
        lines_kernel,
        grid=(ROWS // 2,),
        in_specs=[spec, spec, pl.BlockSpec((2, N, N), lambda i: (0, 0, 0))],
        out_specs=pl.BlockSpec((HALF * ROWS, 128), lambda i: (0, 0)),
        out_shape=jax.ShapeDtypeStruct((HALF * ROWS, 128), f32),
        name="lines",
    )(one, two, jnp.asarray(split_table(forward_table)))


def planes_kernel(line_ref, in_ref, forward_ref, inverse_ref, slope_ref, inverse_t_ref, slope_t_ref, out_ref):
    mask = low_lanes((N, 128))
    tiles = [in_ref[:, g].reshape(N, 128) for g in range(4)]
    swapped = [pltpu.roll(tile, DEPTH, 1) for tile in tiles]
    first = [jnp.where(mask, tiles[g], swapped[g + 1]) for g in (0, 2)]
    second = [jnp.where(mask, swapped[g], tiles[g + 1]) for g in (0, 2)]
    stacked = jnp.concatenate(
        [jnp.concatenate(first, axis=1), jnp.concatenate(second, axis=1)], axis=0
    )
    forward = (forward_ref[0], forward_ref[1])
    inverse = (inverse_ref[0], inverse_ref[1])
    slope = (slope_ref[0], slope_ref[1])
    inverse_t = (inverse_t_ref[0], inverse_t_ref[1])
    slope_t = (slope_t_ref[0], slope_t_ref[1])
    depth = dot3(split(stacked), forward, NT)
    step = 2.0 * np.pi / N
    rows = lax.broadcasted_iota(jnp.int32, (N, N), 0)
    columns = lax.broadcasted_iota(jnp.int32, (N, N), 1)
    wave_rows = jnp.where(rows > HALF, rows - HALF, rows).astype(f32) * step
    wave_columns = jnp.where(columns > HALF, columns - HALF, columns).astype(f32) * step
    plane_square = wave_rows * wave_rows + wave_columns * wave_columns
    filtered = []
    for part in range(2):
        spectrum = dot3(forward, split(depth[part * N : (part + 1) * N]), NN)
        line = line_ref[0] + (HALF if part == 1 else 0) * (line_ref[0] == 0).astype(jnp.int32)
        wave_line = line.astype(f32) * step
        square = plane_square + wave_line * wave_line
        filtered.append(
            jnp.where(square > 0.0, spectrum / jnp.where(square > 0.0, square, 1.0), 0.0)
        )
    stacked = split(jnp.concatenate(filtered, axis=0))
    plain = split(dot3(stacked, inverse, NN))
    sloped = split(dot3(stacked, slope, NN))
    part_of = lambda pair, part: tuple(v[part * N : (part + 1) * N] for v in pair)
    for field, (matrix, values) in enumerate(
        ((inverse_t, plain), (slope_t, plain), (inverse_t, sloped))
    ):
        first = dot3(matrix, part_of(values, 0), NN)
        second = dot3(matrix, part_of(values, 1), NN)
        for g in (0, 2):
            lanes = slice(g * DEPTH, g * DEPTH + 128)
            a, b = first[:, lanes], second[:, lanes]
            even = jnp.where(mask, a, pltpu.roll(b, DEPTH, 1))
            odd = jnp.where(mask, pltpu.roll(a, DEPTH, 1), b)
            out_ref[:, g, field * ROWS : (field + 1) * ROWS, :] = even.reshape(32, ROWS, 128)
            out_ref[:, g + 1, field * ROWS : (field + 1) * ROWS, :] = odd.reshape(32, ROWS, 128)


def planes(line, values):
    whole = pl.BlockSpec(memory_space=pltpu.VMEM)
    tables = [
        jnp.asarray(split_table(t))
        for t in (forward_table, inverse_table, slope_table, inverse_table.T, slope_table.T)
    ]
    return pl.pallas_call(
        planes_kernel,
        in_specs=[pl.BlockSpec(memory_space=pltpu.SMEM)] + [whole] * 6,
        out_specs=whole,
        out_shape=jax.ShapeDtypeStruct((32, 4, 3 * ROWS, 128), f32),
        compiler_params=pltpu.CompilerParams(vmem_limit_bytes=60000 * 1024),
        name="planes",
    )(line, values, *tables)


def fields_kernel(in_ref, inverse_ref, slope_ref, out_ref):
    pair = pl.program_id(0)
    mask = low_lanes((HALF, 128))
    inverse = (inverse_ref[0], inverse_ref[1])
    slope = (slope_ref[0], slope_ref[1])
    for field in range(3):
        start = field * ROWS + 2 * pair
        even = in_ref[pl.ds(start, HALF, stride=3 * ROWS), :]
        odd = in_ref[pl.ds(start + 1, HALF, stride=3 * ROWS), :]
        first = jnp.where(mask, even, pltpu.roll(odd, DEPTH, 1))
        second = jnp.where(mask, pltpu.roll(even, DEPTH, 1), odd)
        stacked = jnp.concatenate([first, second], axis=0)
        table = slope if field == 0 else inverse
        result = dot3(split(stacked), table, TN)
        out_ref[field, 0] = result[:DEPTH]
        out_ref[field, 1] = result[DEPTH:]


def fields(values):
    table = pl.BlockSpec((2, N, N), lambda i: (0, 0, 0))
    return pl.pallas_call(
        fields_kernel,
        grid=(ROWS // 2,),
        in_specs=[pl.BlockSpec((HALF * 3 * ROWS, 128), lambda i: (0, 0)), table, table],
        out_specs=pl.BlockSpec((3, 2, DEPTH, N), lambda i: (0, i, 0, 0)),
        out_shape=jax.ShapeDtypeStruct((3, ROWS, DEPTH, N), f32),
        name="fields",
    )(values, jnp.asarray(split_table(inverse_table)), jnp.asarray(split_table(slope_table)))


def tile_weights(moved):
    weights = []
    for shift in range(5):
        distance = jnp.abs(moved + (shift - 2.0))
        outer = jnp.maximum(2.0 - distance, 0.0)
        inner = jnp.maximum(outer - 1.0, 0.0)
        weights.append(outer * outer * outer - 4.0 * (inner * inner * inner))
    return weights


def deposit_kernel(rows, cells, displacement_ref, field_ref, out_ref, weight_ref, sum_ref, spill_ref):
    for slot, row in enumerate(rows):

        @pl.loop(0, ROWS)
        def _(tile):
            start = pl.multiple_of(tile * 8, 8)
            for axis in range(3):
                moved = (
                    displacement_ref[axis, row, pl.ds(start, 8), :]
                    + field_ref[axis, row, pl.ds(start, 8), :]
                )
                for shift, weight in enumerate(tile_weights(moved)):
                    weight_ref[5 * axis + shift, slot, pl.ds(start, 8), :] = weight

    sublane = lax.broadcasted_iota(jnp.int32, (8, 128), 0)
    for out_row, pairs in enumerate(cells):

        @pl.loop(0, ROWS)
        def _(tile):
            start = pl.multiple_of(tile * 8, 8)
            for half in range(2):
                lanes = slice(half * 128, half * 128 + 128)
                total = None
                for slot, shift_row in pairs:
                    get = lambda index: weight_ref[index, slot, pl.ds(start, 8), lanes]
                    line_weights = [get(s) for s in range(5)]
                    row_weight = get(5 + shift_row)
                    terms = []
                    for shift_depth in range(5):
                        plane = row_weight * get(10 + shift_depth)
                        terms.append([plane * w for w in line_weights])
                    if total is None:
                        total = terms
                    else:
                        total = [[a + b for a, b in zip(x, y)] for x, y in zip(total, terms)]
                for shift_line in range(5):
                    up2 = pltpu.roll(total[0][shift_line], 2, 0)
                    up1 = pltpu.roll(total[1][shift_line], 1, 0)
                    down1 = pltpu.roll(total[3][shift_line], 7, 0)
                    down2 = pltpu.roll(total[4][shift_line], 6, 0)
                    main = (
                        total[2][shift_line]
                        + jnp.where(sublane >= 2, up2, 0.0)
                        + jnp.where(sublane >= 1, up1, 0.0)
                        + jnp.where(sublane < 7, down1, 0.0)
                        + jnp.where(sublane < 6, down2, 0.0)
                    )
                    spill = jnp.where(
                        sublane < 2,
                        up2 + jnp.where(sublane < 1, up1, 0.0),
                        down2 + jnp.where(sublane >= 7, down1, 0.0),
                    )
                    sum_ref[shift_line, pl.ds(start, 8), lanes] = main
                    spill_ref[shift_line, pl.ds(start + 8, 8), lanes] = spill

        for shift_line in range(5):
            spill_ref[shift_line, 0:8, :] = jnp.zeros((8, N), f32)
            spill_ref[shift_line, 72:80, :] = jnp.zeros((8, N), f32)
            spill_ref[shift_line, 80:88, :] = spill_ref[shift_line, 8:16, :]
            sum_ref[shift_line, 64:72, :] = jnp.zeros((8, N), f32)
        wide = lax.broadcasted_iota(jnp.int32, (8, N), 0)

        @pl.loop(0, ROWS + 1)
        def _(tile):
            start = pl.multiple_of(tile * 8, 8)
            result = jnp.zeros((8, N), f32)
            for shift_line in range(5):
                value = sum_ref[shift_line, pl.ds(start, 8), :]
                value = value + jnp.where(wide < 2, spill_ref[shift_line, pl.ds(start, 8), :], 0.0)
                value = value + jnp.where(
                    wide >= 6, spill_ref[shift_line, pl.ds(start + 16, 8), :], 0.0
                )
                shift = (2 - shift_line) % N
                result = result + (pltpu.roll(value, shift, 1) if shift else value)
            out_ref[out_row, pl.ds(start, 8), :] = result * (1.0 / 216.0)


def deposit(displacement, moved, rows, cells, name):
    whole = pl.BlockSpec(memory_space=pltpu.VMEM)
    return pl.pallas_call(
        functools.partial(deposit_kernel, rows, cells),
        in_specs=[whole, whole],
        out_specs=whole,
        out_shape=jax.ShapeDtypeStruct((len(cells), DEPTH + 8, N), f32),
        scratch_shapes=[
            pltpu.VMEM((15, len(rows), DEPTH, N), f32),
            pltpu.VMEM((5, DEPTH + 8, N), f32),
            pltpu.VMEM((5, DEPTH + 24, N), f32),
        ],
        compiler_params=pltpu.CompilerParams(vmem_limit_bytes=60000 * 1024),
        name=name,
    )(displacement, moved)


def reach(cells, rows):
    return tuple(
        tuple((slot, row + 2 - cell) for slot, row in enumerate(rows) if 0 <= row + 2 - cell < 5)
        for cell in cells
    )


def sum_kernel(inner_ref, low_ref, high_ref, left_ref, right_ref, out_ref):
    for row in range(ROWS):
        value = inner_ref[row, :DEPTH, :] - 1.0
        if row < 2:
            value = value + low_ref[row, :DEPTH, :]
        if row >= ROWS - 2:
            value = value + high_ref[row - ROWS + 2, :DEPTH, :]
        sub = lax.broadcasted_iota(jnp.int32, (8, N), 0)
        out_ref[row, 0:8, :] = value[0:8] + jnp.where(sub < 2, left_ref[row], 0.0)
        out_ref[row, 8:56, :] = value[8:56]
        out_ref[row, 56:64, :] = value[56:64] + jnp.where(sub >= 6, right_ref[row], 0.0)


def local(hessian_one, hessian_two, displacement):
    size_y, size_z = lax.axis_size("gy"), lax.axis_size("gz")
    line = lax.axis_index("gy") * size_z + lax.axis_index("gz")
    both = ("gy", "gz")
    spectra = lines(hessian_one, hessian_two).reshape(HALF, ROWS, 128)
    spectra = lax.all_to_all(spectra, both, split_axis=0, concat_axis=0, tiled=True)
    returned = planes(line.astype(jnp.int32).reshape(1), spectra.reshape(32, 4, ROWS, 128))
    returned = returned.reshape(HALF, 3 * ROWS, 128)
    returned = lax.all_to_all(returned, both, split_axis=0, concat_axis=0, tiled=True)
    psi = fields(returned.reshape(HALF * 3 * ROWS, 128))
    edge = (0, 1, ROWS - 2, ROWS - 1)
    halo = deposit(displacement, psi, edge, reach((-2, -1, ROWS, ROWS + 1), edge), "edges")
    up = [(i, (i + 1) % size_y) for i in range(size_y)]
    down = [(j, i) for i, j in up]
    low = lax.ppermute(halo[2:], "gy", up)
    high = lax.ppermute(halo[:2], "gy", down)
    every = tuple(range(ROWS))
    inner = deposit(displacement, psi, every, reach(every, every), "inner")
    side = inner[:, DEPTH:] + jnp.concatenate(
        [low[:, DEPTH:], jnp.zeros((ROWS - 4, 8, N), f32), high[:, DEPTH:]], axis=0
    )
    up = [(i, (i + 1) % size_z) for i in range(size_z)]
    down = [(j, i) for i, j in up]
    left = lax.ppermute(side, "gz", up)
    right = lax.ppermute(side, "gz", down)
    whole = pl.BlockSpec(memory_space=pltpu.VMEM)
    density = pl.pallas_call(
        sum_kernel,
        in_specs=[whole] * 5,
        out_specs=whole,
        out_shape=jax.ShapeDtypeStruct((ROWS, DEPTH, N), f32),
        name="total",
    )(inner, low, high, left, right)
    return psi, density


def solution(mesh):
    in_specs = (P(None, "gy", "gz", None), P(None, "gy", "gz", None), P(None, "gy", "gz", None))
    out_specs = (P(None, "gy", "gz", None), P("gy", "gz", None))
    return jax.shard_map(local, mesh=mesh, in_specs=in_specs, out_specs=out_specs, check_vma=False)
```

```python
import functools

import jax
import jax.numpy as jnp
import numpy as np
from jax import lax
from jax.experimental import pallas as pl
from jax.experimental.pallas import tpu as pltpu
from jax.sharding import PartitionSpec as P

N = 256
HALF = N // 2
ROWS = 8
DEPTH = 64
det_weight = -1.0 / 3.0
mixed_weight = 10.0 / 21.0
f32 = jnp.float32
bf16 = jnp.bfloat16


def split_table(table):
    high = table.astype(np.float32).astype(jnp.bfloat16)
    low = (table - high.astype(np.float64)).astype(np.float32).astype(jnp.bfloat16)
    return np.stack([high, low])


def wave_index():
    order = np.arange(N)
    return np.where(order <= HALF, order, order - HALF)


def real_tables():
    order = np.arange(N)
    wave = wave_index()
    is_sin = order > HALF
    angle = 2.0 * np.pi / N * (wave[:, None] * np.arange(N)[None, :] % N)
    cosine, sine = np.cos(angle), np.sin(angle)
    forward = np.where(is_sin[:, None], sine, cosine)
    single = (order == 0) | (order == HALF)
    weight = np.where(single, 1.0, 2.0)[:, None] / N
    inverse = weight * forward
    number = (2.0 * np.pi / N * np.where(single, 0, wave))[:, None]
    slope = weight * number * np.where(is_sin[:, None], cosine, -sine)
    return forward, inverse, slope


forward_table, inverse_table, slope_table = real_tables()


def split(value):
    high = value.astype(bf16)
    return high, (value - high.astype(f32)).astype(bf16)


def dot3(left, right, dims):
    (left_high, left_low), (right_high, right_low) = left, right
    product = functools.partial(
        lax.dot_general, dimension_numbers=(dims, ((), ())), preferred_element_type=f32
    )
    return product(left_high, right_high) + (
        product(left_high, right_low) + product(left_low, right_high)
    )


NN = ((1,), (0,))
NT = ((1,), (1,))
TN = ((0,), (0,))


def low_lanes(shape):
    return lax.broadcasted_iota(jnp.int32, shape, len(shape) - 1) < DEPTH


def source_term(one, two):
    primary = [one[c].astype(f32) for c in range(6)]
    secondary = [two[c].astype(f32) for c in range(6)]
    determinant = (
        primary[0] * (primary[1] * primary[2] - primary[5] * primary[5])
        - primary[3] * (primary[3] * primary[2] - primary[5] * primary[4])
        + primary[4] * (primary[3] * primary[5] - primary[1] * primary[4])
    )
    mixed = 0.5 * (
        secondary[0] * (primary[1] + primary[2])
        + secondary[1] * (primary[0] + primary[2])
        + secondary[2] * (primary[0] + primary[1])
    )
    mixed = mixed - (
        secondary[3] * primary[3] + secondary[4] * primary[4] + secondary[5] * primary[5]
    )
    return det_weight * determinant + mixed_weight * mixed


def lines_kernel(one_ref, two_ref, table_ref, out_ref):
    pair = pl.program_id(0)
    source = jnp.concatenate(
        [
            source_term(
                [one_ref[c, row] for c in range(6)], [two_ref[c, row] for c in range(6)]
            )
            for row in range(2)
        ],
        axis=0,
    )
    result = dot3((table_ref[0], table_ref[1]), split(source), NT)
    first, second = result[:HALF], result[HALF:]
    mask = low_lanes((HALF, 128))
    out_ref[pl.ds(2 * pair, HALF, stride=ROWS), :] = jnp.where(
        mask, first, pltpu.roll(second, DEPTH, 1)
    )
    out_ref[pl.ds(2 * pair + 1, HALF, stride=ROWS), :] = jnp.where(
        mask, pltpu.roll(first, DEPTH, 1), second
    )


def lines(one, two):
    spec = pl.BlockSpec((6, 2, DEPTH, N), lambda i: (0, i, 0, 0))
    return pl.pallas_call(
        lines_kernel,
        grid=(ROWS // 2,),
        in_specs=[spec, spec, pl.BlockSpec((2, N, N), lambda i: (0, 0, 0))],
        out_specs=pl.BlockSpec((HALF * ROWS, 128), lambda i: (0, 0)),
        out_shape=jax.ShapeDtypeStruct((HALF * ROWS, 128), f32),
        name="lines",
    )(one, two, jnp.asarray(split_table(forward_table)))


def planes_kernel(line_ref, in_ref, forward_ref, inverse_ref, slope_ref, inverse_t_ref, slope_t_ref, out_ref):
    mask = low_lanes((N, 128))
    tiles = [in_ref[:, g].reshape(N, 128) for g in range(4)]
    swapped = [pltpu.roll(tile, DEPTH, 1) for tile in tiles]
    first = [jnp.where(mask, tiles[g], swapped[g + 1]) for g in (0, 2)]
    second = [jnp.where(mask, swapped[g], tiles[g + 1]) for g in (0, 2)]
    stacked = jnp.concatenate(
        [jnp.concatenate(first, axis=1), jnp.concatenate(second, axis=1)], axis=0
    )
    forward = (forward_ref[0], forward_ref[1])
    inverse = (inverse_ref[0], inverse_ref[1])
    slope = (slope_ref[0], slope_ref[1])
    inverse_t = (inverse_t_ref[0], inverse_t_ref[1])
    slope_t = (slope_t_ref[0], slope_t_ref[1])
    depth = dot3(split(stacked), forward, NT)
    step = 2.0 * np.pi / N
    rows = lax.broadcasted_iota(jnp.int32, (N, N), 0)
    columns = lax.broadcasted_iota(jnp.int32, (N, N), 1)
    wave_rows = jnp.where(rows > HALF, rows - HALF, rows).astype(f32) * step
    wave_columns = jnp.where(columns > HALF, columns - HALF, columns).astype(f32) * step
    plane_square = wave_rows * wave_rows + wave_columns * wave_columns
    filtered = []
    for part in range(2):
        spectrum = dot3(forward, split(depth[part * N : (part + 1) * N]), NN)
        line = line_ref[0] + (HALF if part == 1 else 0) * (line_ref[0] == 0).astype(jnp.int32)
        wave_line = line.astype(f32) * step
        square = plane_square + wave_line * wave_line
        filtered.append(
            jnp.where(square > 0.0, spectrum / jnp.where(square > 0.0, square, 1.0), 0.0)
        )
    stacked = split(jnp.concatenate(filtered, axis=0))
    plain = split(dot3(stacked, inverse, NN))
    sloped = split(dot3(stacked, slope, NN))
    part_of = lambda pair, part: tuple(v[part * N : (part + 1) * N] for v in pair)
    for field, (matrix, values) in enumerate(
        ((inverse_t, plain), (slope_t, plain), (inverse_t, sloped))
    ):
        first = dot3(matrix, part_of(values, 0), NN)
        second = dot3(matrix, part_of(values, 1), NN)
        for g in (0, 2):
            lanes = slice(g * DEPTH, g * DEPTH + 128)
            a, b = first[:, lanes], second[:, lanes]
            even = jnp.where(mask, a, pltpu.roll(b, DEPTH, 1))
            odd = jnp.where(mask, pltpu.roll(a, DEPTH, 1), b)
            out_ref[:, g, field * ROWS : (field + 1) * ROWS, :] = even.reshape(32, ROWS, 128)
            out_ref[:, g + 1, field * ROWS : (field + 1) * ROWS, :] = odd.reshape(32, ROWS, 128)


def planes(line, values):
    whole = pl.BlockSpec(memory_space=pltpu.VMEM)
    tables = [
        jnp.asarray(split_table(t))
        for t in (forward_table, inverse_table, slope_table, inverse_table.T, slope_table.T)
    ]
    return pl.pallas_call(
        planes_kernel,
        in_specs=[pl.BlockSpec(memory_space=pltpu.SMEM)] + [whole] * 6,
        out_specs=whole,
        out_shape=jax.ShapeDtypeStruct((32, 4, 3 * ROWS, 128), f32),
        compiler_params=pltpu.CompilerParams(vmem_limit_bytes=60000 * 1024),
        name="planes",
    )(line, values, *tables)


PAD = 8
HELD = DEPTH + 3 * PAD
EDGE_ROWS = (0, 1, ROWS - 2, ROWS - 1)
EVERY_ROW = tuple(range(ROWS))


def tile_weights(moved):
    weights = []
    for shift in range(5):
        distance = jnp.abs(moved + (shift - 2.0))
        outer = jnp.maximum(2.0 - distance, 0.0)
        inner = jnp.maximum(1.0 - distance, 0.0)
        weights.append(outer * outer * outer - 4.0 * (inner * inner * inner))
    return weights


def row_pair(row, slots, in_ref, displacement_ref, inverse, slope, psi_ref, weight_ref):
    mask = low_lanes((HALF, 128))
    for slot in slots:
        zeros = jnp.zeros((15, 2, PAD, 128), f32)
        weight_ref[slot, :, :, 0:PAD, :] = zeros
        weight_ref[slot, :, :, PAD + DEPTH : 2 * PAD + DEPTH, :] = zeros
    for field in range(3):
        start = field * ROWS + row
        even = in_ref[pl.ds(start, HALF, stride=3 * ROWS), :]
        odd = in_ref[pl.ds(start + 1, HALF, stride=3 * ROWS), :]
        first = jnp.where(mask, even, pltpu.roll(odd, DEPTH, 1))
        second = jnp.where(mask, pltpu.roll(even, DEPTH, 1), odd)
        stacked = jnp.concatenate([first, second], axis=0)
        result = dot3(split(stacked), slope if field == 0 else inverse, TN)
        for part, slot in enumerate(slots):
            values = result[part * DEPTH : (part + 1) * DEPTH]
            psi_ref[slot, field] = values
            for tile in range(DEPTH // 8):
                for half in range(2):
                    lanes = slice(half * 128, half * 128 + 128)
                    rows = slice(tile * 8, tile * 8 + 8)
                    moved = displacement_ref[field, row + part, rows, lanes] + values[rows, lanes]
                    for shift, weight in enumerate(tile_weights(moved)):
                        place = slice(PAD + tile * 8, PAD + tile * 8 + 8)
                        weight_ref[slot, 5 * field + shift, half, place, :] = weight
                        if tile == 0:
                            weight_ref[slot, 5 * field + shift, half, HELD - PAD : HELD, :] = weight


def line_sums(carry_ref):
    lane = lax.broadcasted_iota(jnp.int32, (8, 128), 1)
    low, high = carry_ref[0, 2], carry_ref[1, 2]
    for shift_line in (0, 1, 3, 4):
        move = 2 - shift_line
        a = pltpu.roll(carry_ref[0, shift_line], move % 128, 1)
        b = pltpu.roll(carry_ref[1, shift_line], move % 128, 1)
        wraps = lane < move if move > 0 else lane >= 128 + move
        low = low + jnp.where(wraps, b, a)
        high = high + jnp.where(wraps, a, b)
    return low * (1.0 / 216.0), high * (1.0 / 216.0)


def collect(weight_ref, carry_ref, pairs, out_ref, row):
    def store(start):
        low, high = line_sums(carry_ref)
        out_ref[row, pl.ds(start, 8), 0:128] = low
        out_ref[row, pl.ds(start, 8), 128:256] = high

    @pl.loop(0, DEPTH // 8 + 1)
    def _(tile):
        start = pl.multiple_of(tile * 8, 8)
        store(pl.multiple_of(jnp.maximum(tile - 1, 0) * 8, 8))
        for half in range(2):
            totals = None
            for slot, shift_row in pairs:
                for shift_depth in range(5):
                    where = pl.ds(start + PAD - 2 + shift_depth, 8)
                    get = lambda index: weight_ref[slot, index, half, where, :]
                    plane = get(5 + shift_row) * get(10 + shift_depth)
                    terms = [plane * get(s) for s in range(5)]
                    totals = terms if totals is None else [a + b for a, b in zip(totals, terms)]
            for shift_line in range(5):
                carry_ref[half, shift_line] = totals[shift_line]

    store(DEPTH)


def reach(cells, rows):
    return tuple(
        tuple((slot, row + 2 - cell) for slot, row in enumerate(rows) if 0 <= row + 2 - cell < 5)
        for cell in cells
    )


def edges_kernel(
    in_ref, displacement_ref, inverse_ref, slope_ref,
    psi_out, weight_out, before_ref, after_ref,
    psi_ref, weight_ref, carry_ref, psi_sem, weight_sem,
):
    inverse = (inverse_ref[0], inverse_ref[1])
    slope = (slope_ref[0], slope_ref[1])
    copies = []
    for pair, row in enumerate((0, ROWS - 2)):
        slots = (2 * pair, 2 * pair + 1)
        row_pair(row, slots, in_ref, displacement_ref, inverse, slope, psi_ref, weight_ref)
        for part, slot in enumerate(slots):
            copies.append(
                pltpu.make_async_copy(weight_ref.at[slot], weight_out.at[slot], weight_sem.at[slot])
            )
            copies.append(
                pltpu.make_async_copy(psi_ref.at[slot], psi_out.at[:, row + part], psi_sem.at[slot])
            )
        for copy in copies[-4:]:
            copy.start()
    cells = reach((-2, -1, ROWS, ROWS + 1), EDGE_ROWS)
    for index in range(2):
        collect(weight_ref, carry_ref, cells[index], before_ref, index)
        collect(weight_ref, carry_ref, cells[2 + index], after_ref, index)
    for copy in copies:
        copy.wait()


VMEM = pl.BlockSpec(memory_space=pltpu.VMEM)
ANY = pl.BlockSpec(memory_space=pl.ANY)


def edges(values, displacement, tables):
    halo = jax.ShapeDtypeStruct((2, DEPTH + PAD, N), f32)
    return pl.pallas_call(
        edges_kernel,
        in_specs=[VMEM] * 4,
        out_specs=[ANY, ANY, VMEM, VMEM],
        out_shape=[
            jax.ShapeDtypeStruct((3, ROWS, DEPTH, N), f32),
            jax.ShapeDtypeStruct((4, 15, 2, HELD, 128), f32),
            halo,
            halo,
        ],
        scratch_shapes=[
            pltpu.VMEM((4, 3, DEPTH, N), f32),
            pltpu.VMEM((4, 15, 2, HELD, 128), f32),
            pltpu.VMEM((2, 5, 8, 128), f32),
            pltpu.SemaphoreType.DMA((4,)),
            pltpu.SemaphoreType.DMA((4,)),
        ],
        compiler_params=pltpu.CompilerParams(vmem_limit_bytes=32 << 20),
        name="edges",
    )(values, displacement, *tables)


def inner_kernel(
    in_ref, displacement_ref, inverse_ref, slope_ref, psi_in, weight_in,
    psi_out, out_ref,
    psi_ref, weight_ref, carry_ref, psi_sem, weight_sem,
):
    inverse = (inverse_ref[0], inverse_ref[1])
    slope = (slope_ref[0], slope_ref[1])
    loads = [
        pltpu.make_async_copy(weight_in.at[slot], weight_ref.at[row], weight_sem.at[slot])
        for slot, row in enumerate(EDGE_ROWS)
    ]
    for load in loads:
        load.start()
    copies = []
    for row in (2, 4):
        slots = (row, row + 1)
        row_pair(row, slots, in_ref, displacement_ref, inverse, slope, psi_ref, weight_ref)
        for slot in slots:
            copy = pltpu.make_async_copy(psi_ref.at[slot], psi_out.at[:, slot], psi_sem.at[slot])
            copy.start()
            copies.append(copy)
    for load in loads:
        load.wait()
    for row, pairs in enumerate(reach(EVERY_ROW, EVERY_ROW)):
        collect(weight_ref, carry_ref, pairs, out_ref, row)
    for copy in copies:
        copy.wait()


def inner(values, displacement, tables, psi, weights):
    return pl.pallas_call(
        inner_kernel,
        in_specs=[VMEM] * 4 + [ANY, ANY],
        out_specs=[ANY, VMEM],
        out_shape=[
            jax.ShapeDtypeStruct((3, ROWS, DEPTH, N), f32),
            jax.ShapeDtypeStruct((ROWS, DEPTH + PAD, N), f32),
        ],
        scratch_shapes=[
            pltpu.VMEM((ROWS, 3, DEPTH, N), f32),
            pltpu.VMEM((ROWS, 15, 2, HELD, 128), f32),
            pltpu.VMEM((2, 5, 8, 128), f32),
            pltpu.SemaphoreType.DMA((ROWS,)),
            pltpu.SemaphoreType.DMA((4,)),
        ],
        input_output_aliases={4: 0},
        compiler_params=pltpu.CompilerParams(vmem_limit_bytes=32 << 20),
        name="inner",
    )(values, displacement, *tables, psi, weights)


def sum_kernel(inner_ref, low_ref, high_ref, left_ref, right_ref, out_ref):
    for row in range(ROWS):
        value = inner_ref[row, :DEPTH, :] - 1.0
        if row < 2:
            value = value + low_ref[row, :DEPTH, :]
        if row >= ROWS - 2:
            value = value + high_ref[row - ROWS + 2, :DEPTH, :]
        sub = lax.broadcasted_iota(jnp.int32, (8, N), 0)
        out_ref[row, 0:8, :] = value[0:8] + jnp.where(sub < 2, left_ref[row], 0.0)
        out_ref[row, 8:56, :] = value[8:56]
        out_ref[row, 56:64, :] = value[56:64] + jnp.where(sub >= 6, right_ref[row], 0.0)


def local(hessian_one, hessian_two, displacement):
    size_y, size_z = lax.axis_size("gy"), lax.axis_size("gz")
    line = lax.axis_index("gy") * size_z + lax.axis_index("gz")
    both = ("gy", "gz")
    spectra = lines(hessian_one, hessian_two).reshape(HALF, ROWS, 128)
    spectra = lax.all_to_all(spectra, both, split_axis=0, concat_axis=0, tiled=True)
    returned = planes(line.astype(jnp.int32).reshape(1), spectra.reshape(32, 4, ROWS, 128))
    returned = returned.reshape(HALF, 3 * ROWS, 128)
    returned = lax.all_to_all(returned, both, split_axis=0, concat_axis=0, tiled=True)
    returned = returned.reshape(HALF * 3 * ROWS, 128)
    tables = [jnp.asarray(split_table(t)) for t in (inverse_table, slope_table)]
    psi, weights, before, after = edges(returned, displacement, tables)
    up = [(i, (i + 1) % size_y) for i in range(size_y)]
    down = [(j, i) for i, j in up]
    low = lax.ppermute(after, "gy", up)
    high = lax.ppermute(before, "gy", down)
    psi, cells = inner(returned, displacement, tables, psi, weights)
    side = cells[:, DEPTH:] + jnp.concatenate(
        [low[:, DEPTH:], jnp.zeros((ROWS - 4, 8, N), f32), high[:, DEPTH:]], axis=0
    )
    up = [(i, (i + 1) % size_z) for i in range(size_z)]
    down = [(j, i) for i, j in up]
    left = lax.ppermute(side, "gz", up)
    right = lax.ppermute(side, "gz", down)
    whole = pl.BlockSpec(memory_space=pltpu.VMEM)
    density = pl.pallas_call(
        sum_kernel,
        in_specs=[whole] * 5,
        out_specs=whole,
        out_shape=jax.ShapeDtypeStruct((ROWS, DEPTH, N), f32),
        name="total",
    )(cells, low, high, left, right)
    return psi, density


def solution(mesh):
    in_specs = (P(None, "gy", "gz", None), P(None, "gy", "gz", None), P(None, "gy", "gz", None))
    out_specs = (P(None, "gy", "gz", None), P("gy", "gz", None))
    return jax.shard_map(local, mesh=mesh, in_specs=in_specs, out_specs=out_specs, check_vma=False)
```

```python
import functools

import jax
import jax.numpy as jnp
import numpy as np
from jax import lax
from jax.experimental import pallas as pl
from jax.experimental.pallas import tpu as pltpu
from jax.sharding import PartitionSpec as P

N = 256
HALF = N // 2
ROWS = 8
DEPTH = 64
det_weight = -1.0 / 3.0
mixed_weight = 10.0 / 21.0
f32 = jnp.float32
bf16 = jnp.bfloat16


def split_table(table):
    high = table.astype(np.float32).astype(jnp.bfloat16)
    low = (table - high.astype(np.float64)).astype(np.float32).astype(jnp.bfloat16)
    return np.stack([high, low])


def wave_index():
    order = np.arange(N)
    return np.where(order <= HALF, order, order - HALF)


def real_tables():
    order = np.arange(N)
    wave = wave_index()
    is_sin = order > HALF
    angle = 2.0 * np.pi / N * (wave[:, None] * np.arange(N)[None, :] % N)
    cosine, sine = np.cos(angle), np.sin(angle)
    forward = np.where(is_sin[:, None], sine, cosine)
    single = (order == 0) | (order == HALF)
    weight = np.where(single, 1.0, 2.0)[:, None] / N
    inverse = weight * forward
    number = (2.0 * np.pi / N * np.where(single, 0, wave))[:, None]
    slope = weight * number * np.where(is_sin[:, None], cosine, -sine)
    return forward, inverse, slope


forward_table, inverse_table, slope_table = real_tables()


def split(value):
    high = value.astype(bf16)
    return high, (value - high.astype(f32)).astype(bf16)


def dot3(left, right, dims):
    (left_high, left_low), (right_high, right_low) = left, right
    product = functools.partial(
        lax.dot_general, dimension_numbers=(dims, ((), ())), preferred_element_type=f32
    )
    return product(left_high, right_high) + (
        product(left_high, right_low) + product(left_low, right_high)
    )


NN = ((1,), (0,))
NT = ((1,), (1,))
TN = ((0,), (0,))


def low_lanes(shape):
    return lax.broadcasted_iota(jnp.int32, shape, len(shape) - 1) < DEPTH


def source_term(one, two):
    primary = [one[c].astype(f32) for c in range(6)]
    secondary = [two[c].astype(f32) for c in range(6)]
    determinant = (
        primary[0] * (primary[1] * primary[2] - primary[5] * primary[5])
        - primary[3] * (primary[3] * primary[2] - primary[5] * primary[4])
        + primary[4] * (primary[3] * primary[5] - primary[1] * primary[4])
    )
    mixed = 0.5 * (
        secondary[0] * (primary[1] + primary[2])
        + secondary[1] * (primary[0] + primary[2])
        + secondary[2] * (primary[0] + primary[1])
    )
    mixed = mixed - (
        secondary[3] * primary[3] + secondary[4] * primary[4] + secondary[5] * primary[5]
    )
    return det_weight * determinant + mixed_weight * mixed


def lines_kernel(one_in, two_in, table_in, out_ref, one_ref, two_ref, table_ref, sem):
    table_copy = pltpu.make_async_copy(table_in, table_ref, sem.at[ROWS])
    table_copy.start()
    copies = []
    for pair in range(ROWS // 2):
        rows = slice(2 * pair, 2 * pair + 2)
        for index, (source, target) in enumerate(((one_in, one_ref), (two_in, two_ref))):
            copy = pltpu.make_async_copy(
                source.at[:, rows], target.at[:, rows], sem.at[2 * pair + index]
            )
            copy.start()
            copies.append(copy)
    mask = low_lanes((HALF, 128))
    table_copy.wait()
    for pair in range(ROWS // 2):
        copies[2 * pair].wait()
        copies[2 * pair + 1].wait()
        source = jnp.concatenate(
            [
                source_term(
                    [one_ref[c, row] for c in range(6)], [two_ref[c, row] for c in range(6)]
                )
                for row in (2 * pair, 2 * pair + 1)
            ],
            axis=0,
        )
        result = dot3((table_ref[0], table_ref[1]), split(source), NT)
        first, second = result[:HALF], result[HALF:]
        out_ref[pl.ds(2 * pair, HALF, stride=ROWS), :] = jnp.where(
            mask, first, pltpu.roll(second, DEPTH, 1)
        )
        out_ref[pl.ds(2 * pair + 1, HALF, stride=ROWS), :] = jnp.where(
            mask, pltpu.roll(first, DEPTH, 1), second
        )


def lines(one, two):
    far = pl.BlockSpec(memory_space=pltpu.HBM)
    return pl.pallas_call(
        lines_kernel,
        in_specs=[far] * 3,
        out_specs=pl.BlockSpec(memory_space=pltpu.VMEM),
        out_shape=jax.ShapeDtypeStruct((HALF * ROWS, 128), f32),
        scratch_shapes=[
            pltpu.VMEM((6, ROWS, DEPTH, N), bf16),
            pltpu.VMEM((6, ROWS, DEPTH, N), bf16),
            pltpu.VMEM((2, N, N), bf16),
            pltpu.SemaphoreType.DMA((ROWS + 1,)),
        ],
        compiler_params=pltpu.CompilerParams(vmem_limit_bytes=60 << 20),
        name="lines",
    )(one, two, jnp.asarray(split_table(forward_table)))


def planes_kernel(in_ref, forward_ref, inverse_ref, slope_ref, inverse_t_ref, slope_t_ref, out_ref):
    mask = low_lanes((N, 128))
    tiles = [in_ref[:, g].reshape(N, 128) for g in range(4)]
    swapped = [pltpu.roll(tile, DEPTH, 1) for tile in tiles]
    first = [jnp.where(mask, tiles[g], swapped[g + 1]) for g in (0, 2)]
    second = [jnp.where(mask, swapped[g], tiles[g + 1]) for g in (0, 2)]
    stacked = jnp.concatenate(
        [jnp.concatenate(first, axis=1), jnp.concatenate(second, axis=1)], axis=0
    )
    forward = (forward_ref[0], forward_ref[1])
    inverse = (inverse_ref[0], inverse_ref[1])
    slope = (slope_ref[0], slope_ref[1])
    inverse_t = (inverse_t_ref[0], inverse_t_ref[1])
    slope_t = (slope_t_ref[0], slope_t_ref[1])
    depth = dot3(split(stacked), forward, NT)
    step = 2.0 * np.pi / N
    rows = lax.broadcasted_iota(jnp.int32, (N, N), 0)
    columns = lax.broadcasted_iota(jnp.int32, (N, N), 1)
    wave_rows = jnp.where(rows > HALF, rows - HALF, rows).astype(f32) * step
    wave_columns = jnp.where(columns > HALF, columns - HALF, columns).astype(f32) * step
    plane_square = wave_rows * wave_rows + wave_columns * wave_columns
    first_line = lax.axis_index("gy") * lax.axis_size("gz") + lax.axis_index("gz")
    filtered = []
    for part in range(2):
        spectrum = dot3(forward, split(depth[part * N : (part + 1) * N]), NN)
        line = first_line + (HALF if part == 1 else 0) * (first_line == 0).astype(jnp.int32)
        wave_line = line.astype(f32) * step
        square = plane_square + wave_line * wave_line
        filtered.append(
            jnp.where(square > 0.0, spectrum / jnp.where(square > 0.0, square, 1.0), 0.0)
        )
    stacked = split(jnp.concatenate(filtered, axis=0))
    plain = split(dot3(stacked, inverse, NN))
    sloped = split(dot3(stacked, slope, NN))
    part_of = lambda pair, part: tuple(v[part * N : (part + 1) * N] for v in pair)
    for field, (matrix, values) in enumerate(
        ((inverse_t, plain), (slope_t, plain), (inverse_t, sloped))
    ):
        first = dot3(matrix, part_of(values, 0), NN)
        second = dot3(matrix, part_of(values, 1), NN)
        for g in (0, 2):
            lanes = slice(g * DEPTH, g * DEPTH + 128)
            a, b = first[:, lanes], second[:, lanes]
            even = jnp.where(mask, a, pltpu.roll(b, DEPTH, 1))
            odd = jnp.where(mask, pltpu.roll(a, DEPTH, 1), b)
            out_ref[:, g, field * ROWS : (field + 1) * ROWS, :] = even.reshape(32, ROWS, 128)
            out_ref[:, g + 1, field * ROWS : (field + 1) * ROWS, :] = odd.reshape(32, ROWS, 128)


def planes(values):
    whole = pl.BlockSpec(memory_space=pltpu.VMEM)
    tables = [
        jnp.asarray(split_table(t))
        for t in (forward_table, inverse_table, slope_table, inverse_table.T, slope_table.T)
    ]
    return pl.pallas_call(
        planes_kernel,
        in_specs=[whole] * 6,
        out_specs=whole,
        out_shape=jax.ShapeDtypeStruct((32, 4, 3 * ROWS, 128), f32),
        compiler_params=pltpu.CompilerParams(vmem_limit_bytes=24 << 20),
        name="planes",
    )(values, *tables)


PAD = 8
HELD = DEPTH + 3 * PAD
EDGE_ROWS = (0, 1, ROWS - 2, ROWS - 1)
EVERY_ROW = tuple(range(ROWS))


def tile_weights(moved):
    weights = []
    for shift in range(5):
        offset = moved + (shift - 2.0) if shift != 2 else moved
        outer = jnp.maximum(2.0 - jnp.abs(offset), 0.0)
        weights.append(
            jnp.minimum(4.0 - 3.0 * ((offset * offset) * outer), (outer * outer) * outer)
        )
    return weights


def row_pair(row, slots, in_ref, displacement_ref, inverse, slope, psi_ref, weight_ref):
    mask = low_lanes((HALF, 128))
    for slot in slots:
        zeros = jnp.zeros((15, 2, PAD, 128), f32)
        weight_ref[slot, :, :, 0:PAD, :] = zeros
        weight_ref[slot, :, :, PAD + DEPTH : 2 * PAD + DEPTH, :] = zeros
    for field in range(3):
        start = field * ROWS + row
        even = in_ref[pl.ds(start, HALF, stride=3 * ROWS), :]
        odd = in_ref[pl.ds(start + 1, HALF, stride=3 * ROWS), :]
        first = jnp.where(mask, even, pltpu.roll(odd, DEPTH, 1))
        second = jnp.where(mask, pltpu.roll(even, DEPTH, 1), odd)
        stacked = jnp.concatenate([first, second], axis=0)
        result = dot3(split(stacked), slope if field == 0 else inverse, TN)
        for part, slot in enumerate(slots):
            values = result[part * DEPTH : (part + 1) * DEPTH]
            psi_ref[slot, field] = values
            for tile in range(DEPTH // 8):
                for half in range(2):
                    lanes = slice(half * 128, half * 128 + 128)
                    rows = slice(tile * 8, tile * 8 + 8)
                    moved = displacement_ref[field, row + part, rows, lanes] + values[rows, lanes]
                    for shift, weight in enumerate(tile_weights(moved)):
                        place = slice(PAD + tile * 8, PAD + tile * 8 + 8)
                        weight_ref[slot, 5 * field + shift, half, place, :] = weight
                        if tile == 0:
                            weight_ref[slot, 5 * field + shift, half, HELD - PAD : HELD, :] = weight


def line_sums(carry_ref):
    lane = lax.broadcasted_iota(jnp.int32, (8, 128), 1)
    low, high = carry_ref[0, 2], carry_ref[1, 2]
    for shift_line in (0, 1, 3, 4):
        move = 2 - shift_line
        a = pltpu.roll(carry_ref[0, shift_line], move % 128, 1)
        b = pltpu.roll(carry_ref[1, shift_line], move % 128, 1)
        wraps = lane < move if move > 0 else lane >= 128 + move
        low = low + jnp.where(wraps, b, a)
        high = high + jnp.where(wraps, a, b)
    return low * (1.0 / 216.0), high * (1.0 / 216.0)


def collect(carry_ref, pairs, out_ref, row):
    def store(start):
        low, high = line_sums(carry_ref)
        out_ref[row, pl.ds(start, 8), 0:128] = low
        out_ref[row, pl.ds(start, 8), 128:256] = high

    @pl.loop(0, DEPTH // 8 + 1)
    def _(tile):
        start = pl.multiple_of(tile * 8, 8)
        store(pl.multiple_of(jnp.maximum(tile - 1, 0) * 8, 8))
        for half in range(2):
            totals = None
            for (weight_ref, slot), shift_row in pairs:
                terms = []
                for shift_depth in range(5):
                    where = pl.ds(start + PAD - 2 + shift_depth, 8)
                    get = lambda index: weight_ref[slot, index, half, where, :]
                    plane = get(5 + shift_row) * get(10 + shift_depth)
                    terms.append([plane * get(s) for s in range(5)])
                sums = [(a + b) + (c + d) + e for a, b, c, d, e in zip(*terms)]
                totals = sums if totals is None else [a + b for a, b in zip(totals, sums)]
            for shift_line in range(5):
                carry_ref[half, shift_line] = totals[shift_line]

    store(DEPTH)


def reach(cell, held):
    return [(held[row], row + 2 - cell) for row in sorted(held) if 0 <= row + 2 - cell < 5]


def edges_kernel(
    in_ref, displacement_ref, inverse_ref, slope_ref,
    psi_out, weight_ref, first_ref, second_ref,
    psi_ref, carry_ref, psi_sem,
):
    inverse = (inverse_ref[0], inverse_ref[1])
    slope = (slope_ref[0], slope_ref[1])
    copies = []
    for pair, row in enumerate((0, ROWS - 2)):
        slots = (2 * pair, 2 * pair + 1)
        row_pair(row, slots, in_ref, displacement_ref, inverse, slope, psi_ref, weight_ref)
        for part, slot in enumerate(slots):
            copy = pltpu.make_async_copy(
                psi_ref.at[slot], psi_out.at[:, row + part], psi_sem.at[slot]
            )
            copy.start()
            copies.append(copy)
    held = {row: (weight_ref, slot) for slot, row in enumerate(EDGE_ROWS)}

    def cells(before_ref, after_ref):
        for index in range(2):
            collect(carry_ref, reach(index - 2, held), before_ref, index)
            collect(carry_ref, reach(ROWS + index, held), after_ref, index)

    odd = lax.axis_index("gy") % 2

    @pl.when(odd == 0)
    def _():
        cells(second_ref, first_ref)

    @pl.when(odd != 0)
    def _():
        cells(first_ref, second_ref)

    for copy in copies:
        copy.wait()


VMEM = pl.BlockSpec(memory_space=pltpu.VMEM)
SMEM = pl.BlockSpec(memory_space=pltpu.SMEM)
ANY = pl.BlockSpec(memory_space=pl.ANY)


def edges(values, displacement, tables):
    halo = jax.ShapeDtypeStruct((2, DEPTH + PAD, N), f32)
    return pl.pallas_call(
        edges_kernel,
        in_specs=[VMEM] * 4,
        out_specs=[ANY, VMEM, VMEM, VMEM],
        out_shape=[
            jax.ShapeDtypeStruct((3, ROWS, DEPTH, N), f32),
            jax.ShapeDtypeStruct((4, 15, 2, HELD, 128), f32),
            halo,
            halo,
        ],
        scratch_shapes=[
            pltpu.VMEM((4, 3, DEPTH, N), f32),
            pltpu.VMEM((2, 5, 8, 128), f32),
            pltpu.SemaphoreType.DMA((4,)),
        ],
        compiler_params=pltpu.CompilerParams(vmem_limit_bytes=16 << 20),
        name="edges",
    )(values, displacement, *tables)


def inner_kernel(
    in_ref, displacement_ref, inverse_ref, slope_ref, psi_in, edge_ref,
    psi_out, out_ref,
    psi_ref, weight_ref, carry_ref, psi_sem,
):
    inverse = (inverse_ref[0], inverse_ref[1])
    slope = (slope_ref[0], slope_ref[1])
    copies = []
    for row in (2, 4):
        slots = (row - 2, row - 1)
        row_pair(row, slots, in_ref, displacement_ref, inverse, slope, psi_ref, weight_ref)
        for slot in slots:
            copy = pltpu.make_async_copy(
                psi_ref.at[slot], psi_out.at[:, slot + 2], psi_sem.at[slot]
            )
            copy.start()
            copies.append(copy)
    held = {row: (edge_ref, slot) for slot, row in enumerate(EDGE_ROWS)}
    held.update({row: (weight_ref, row - 2) for row in range(2, ROWS - 2)})
    for row in range(ROWS):
        collect(carry_ref, reach(row, held), out_ref, row)
    for copy in copies:
        copy.wait()


def inner(values, displacement, tables, psi, weights):
    return pl.pallas_call(
        inner_kernel,
        in_specs=[VMEM] * 4 + [ANY, VMEM],
        out_specs=[ANY, VMEM],
        out_shape=[
            jax.ShapeDtypeStruct((3, ROWS, DEPTH, N), f32),
            jax.ShapeDtypeStruct((ROWS, DEPTH + PAD, N), f32),
        ],
        scratch_shapes=[
            pltpu.VMEM((4, 3, DEPTH, N), f32),
            pltpu.VMEM((4, 15, 2, HELD, 128), f32),
            pltpu.VMEM((2, 5, 8, 128), f32),
            pltpu.SemaphoreType.DMA((4,)),
        ],
        input_output_aliases={4: 0},
        compiler_params=pltpu.CompilerParams(vmem_limit_bytes=20 << 20),
        name="inner",
    )(values, displacement, *tables, psi, weights)


def halos(first_ref, second_ref, where):
    even = lax.axis_index("gy") % 2 == 0
    first, second = first_ref[:, where, :], second_ref[:, where, :]
    return jnp.where(even, second, first), jnp.where(even, first, second)


def sides_kernel(cell_ref, first_ref, second_ref, out_ref):
    low, high = halos(first_ref, second_ref, slice(None))
    side = cell_ref[...]
    out_ref[0:2] = side[0:2] + low
    out_ref[2 : ROWS - 2] = side[2 : ROWS - 2]
    out_ref[ROWS - 2 :] = side[ROWS - 2 :] + high


def sides(cells, first, second):
    last = DEPTH // PAD
    block = lambda rows: pl.BlockSpec((rows, PAD, N), lambda i: (0, last, 0))
    return pl.pallas_call(
        sides_kernel,
        grid=(1,),
        in_specs=[block(ROWS), block(2), block(2)],
        out_specs=pl.BlockSpec((ROWS, PAD, N), lambda i: (0, 0, 0)),
        out_shape=jax.ShapeDtypeStruct((ROWS, PAD, N), f32),
        compiler_params=pltpu.CompilerParams(vmem_limit_bytes=8 << 20),
        name="sides",
    )(cells, first, second)


def sum_kernel(cell_ref, first_ref, second_ref, left_ref, right_ref, out_ref):
    low, high = halos(first_ref, second_ref, slice(0, DEPTH))
    sub = lax.broadcasted_iota(jnp.int32, (PAD, N), 0)
    for row in range(ROWS):
        value = cell_ref[row, :DEPTH, :] - 1.0
        if row < 2:
            value = value + low[row]
        if row >= ROWS - 2:
            value = value + high[row - ROWS + 2]
        out_ref[row, 0:8, :] = value[0:8] + jnp.where(sub < 2, left_ref[row], 0.0)
        out_ref[row, 8:56, :] = value[8:56]
        out_ref[row, 56:64, :] = value[56:64] + jnp.where(sub >= 6, right_ref[row], 0.0)


def total(*parts):
    return pl.pallas_call(
        sum_kernel,
        in_specs=[VMEM] * 5,
        out_specs=VMEM,
        out_shape=jax.ShapeDtypeStruct((ROWS, DEPTH, N), f32),
        compiler_params=pltpu.CompilerParams(vmem_limit_bytes=8 << 20),
        name="total",
    )(*parts)


def local(hessian_one, hessian_two, displacement):
    size_y, size_z = lax.axis_size("gy"), lax.axis_size("gz")
    both = ("gy", "gz")
    spectra = lines(hessian_one, hessian_two).reshape(HALF, ROWS, 128)
    spectra = lax.all_to_all(spectra, both, split_axis=0, concat_axis=0, tiled=True)
    returned = planes(spectra.reshape(32, 4, ROWS, 128))
    returned = returned.reshape(HALF, 3 * ROWS, 128)
    returned = lax.all_to_all(returned, both, split_axis=0, concat_axis=0, tiled=True)
    returned = returned.reshape(HALF * 3 * ROWS, 128)
    tables = [jnp.asarray(split_table(t)) for t in (inverse_table, slope_table)]
    psi, weights, first, second = edges(returned, displacement, tables)
    first = lax.ppermute(first, "gy", [(i, i ^ 1) for i in range(size_y)])
    second = lax.ppermute(
        second, "gy", [(i, (i + (1 if i % 2 else -1)) % size_y) for i in range(size_y)]
    )
    psi, cells = inner(returned, displacement, tables, psi, weights)
    side = sides(cells, first, second)
    up = [(i, (i + 1) % size_z) for i in range(size_z)]
    down = [(j, i) for i, j in up]
    left = lax.ppermute(side, "gz", up)
    right = lax.ppermute(side, "gz", down)
    density = total(cells, first, second, left, right)
    return psi, density


def solution(mesh):
    in_specs = (P(None, "gy", "gz", None), P(None, "gy", "gz", None), P(None, "gy", "gz", None))
    out_specs = (P(None, "gy", "gz", None), P("gy", "gz", None))
    return jax.shard_map(local, mesh=mesh, in_specs=in_specs, out_specs=out_specs, check_vma=False)
```

```python
import functools

import jax
import jax.numpy as jnp
import numpy as np
from jax import lax
from jax.experimental import pallas as pl
from jax.experimental.pallas import tpu as pltpu
from jax.sharding import PartitionSpec as P

N = 256
HALF = N // 2
ROWS = 8
DEPTH = 64
det_weight = -1.0 / 3.0
mixed_weight = 10.0 / 21.0
f32 = jnp.float32
bf16 = jnp.bfloat16


def split_table(table):
    high = table.astype(np.float32).astype(jnp.bfloat16)
    low = (table - high.astype(np.float64)).astype(np.float32).astype(jnp.bfloat16)
    return np.stack([high, low])


def wave_index():
    order = np.arange(N)
    return np.where(order <= HALF, order, order - HALF)


def real_tables():
    order = np.arange(N)
    wave = wave_index()
    is_sin = order > HALF
    angle = 2.0 * np.pi / N * (wave[:, None] * np.arange(N)[None, :] % N)
    cosine, sine = np.cos(angle), np.sin(angle)
    forward = np.where(is_sin[:, None], sine, cosine)
    single = (order == 0) | (order == HALF)
    weight = np.where(single, 1.0, 2.0)[:, None] / N
    inverse = weight * forward
    number = (2.0 * np.pi / N * np.where(single, 0, wave))[:, None]
    slope = weight * number * np.where(is_sin[:, None], cosine, -sine)
    return forward, inverse, slope


forward_table, inverse_table, slope_table = real_tables()


def split(value):
    high = value.astype(bf16)
    return high, (value - high.astype(f32)).astype(bf16)


def dot3(left, right, dims):
    (left_high, left_low), (right_high, right_low) = left, right
    product = functools.partial(
        lax.dot_general, dimension_numbers=(dims, ((), ())), preferred_element_type=f32
    )
    return product(left_high, right_high) + (
        product(left_high, right_low) + product(left_low, right_high)
    )


NN = ((1,), (0,))
NT = ((1,), (1,))
TN = ((0,), (0,))


def low_lanes(shape):
    return lax.broadcasted_iota(jnp.int32, shape, len(shape) - 1) < DEPTH


def source_term(one, two):
    primary = [one[c].astype(f32) for c in range(6)]
    secondary = [two[c].astype(f32) for c in range(6)]
    determinant = (
        primary[0] * (primary[1] * primary[2] - primary[5] * primary[5])
        - primary[3] * (primary[3] * primary[2] - primary[5] * primary[4])
        + primary[4] * (primary[3] * primary[5] - primary[1] * primary[4])
    )
    mixed = 0.5 * (
        secondary[0] * (primary[1] + primary[2])
        + secondary[1] * (primary[0] + primary[2])
        + secondary[2] * (primary[0] + primary[1])
    )
    mixed = mixed - (
        secondary[3] * primary[3] + secondary[4] * primary[4] + secondary[5] * primary[5]
    )
    return det_weight * determinant + mixed_weight * mixed


def lines_kernel(one_in, two_in, table_in, out_ref, one_ref, two_ref, table_ref, sem):
    table_copy = pltpu.make_async_copy(table_in, table_ref, sem.at[ROWS])
    table_copy.start()
    copies = []
    for pair in range(ROWS // 2):
        rows = slice(2 * pair, 2 * pair + 2)
        for index, (source, target) in enumerate(((one_in, one_ref), (two_in, two_ref))):
            copy = pltpu.make_async_copy(
                source.at[:, rows], target.at[:, rows], sem.at[2 * pair + index]
            )
            copy.start()
            copies.append(copy)
    mask = low_lanes((HALF, 128))
    table_copy.wait()
    for pair in range(ROWS // 2):
        copies[2 * pair].wait()
        copies[2 * pair + 1].wait()
        source = jnp.concatenate(
            [
                source_term(
                    [one_ref[c, row] for c in range(6)], [two_ref[c, row] for c in range(6)]
                )
                for row in (2 * pair, 2 * pair + 1)
            ],
            axis=0,
        )
        result = dot3((table_ref[0], table_ref[1]), split(source), NT)
        first, second = result[:HALF], result[HALF:]
        out_ref[pl.ds(2 * pair, HALF, stride=ROWS), :] = jnp.where(
            mask, first, pltpu.roll(second, DEPTH, 1)
        )
        out_ref[pl.ds(2 * pair + 1, HALF, stride=ROWS), :] = jnp.where(
            mask, pltpu.roll(first, DEPTH, 1), second
        )


def lines(one, two):
    far = pl.BlockSpec(memory_space=pltpu.HBM)
    return pl.pallas_call(
        lines_kernel,
        in_specs=[far] * 3,
        out_specs=pl.BlockSpec(memory_space=pltpu.VMEM),
        out_shape=jax.ShapeDtypeStruct((HALF * ROWS, 128), f32),
        scratch_shapes=[
            pltpu.VMEM((6, ROWS, DEPTH, N), bf16),
            pltpu.VMEM((6, ROWS, DEPTH, N), bf16),
            pltpu.VMEM((2, N, N), bf16),
            pltpu.SemaphoreType.DMA((ROWS + 1,)),
        ],
        compiler_params=pltpu.CompilerParams(vmem_limit_bytes=61 << 20),
        name="lines",
    )(one, two, jnp.asarray(split_table(forward_table)))


def planes_kernel(in_ref, forward_ref, inverse_ref, slope_ref, inverse_t_ref, slope_t_ref, out_ref):
    mask = low_lanes((N, 128))
    tiles = [in_ref[:, g].reshape(N, 128) for g in range(4)]
    swapped = [pltpu.roll(tile, DEPTH, 1) for tile in tiles]
    first = [jnp.where(mask, tiles[g], swapped[g + 1]) for g in (0, 2)]
    second = [jnp.where(mask, swapped[g], tiles[g + 1]) for g in (0, 2)]
    stacked = jnp.concatenate(
        [jnp.concatenate(first, axis=1), jnp.concatenate(second, axis=1)], axis=0
    )
    forward = (forward_ref[0], forward_ref[1])
    inverse = (inverse_ref[0], inverse_ref[1])
    slope = (slope_ref[0], slope_ref[1])
    inverse_t = (inverse_t_ref[0], inverse_t_ref[1])
    slope_t = (slope_t_ref[0], slope_t_ref[1])
    depth = dot3(split(stacked), forward, NT)
    step = 2.0 * np.pi / N
    rows = lax.broadcasted_iota(jnp.int32, (N, N), 0)
    columns = lax.broadcasted_iota(jnp.int32, (N, N), 1)
    wave_rows = jnp.where(rows > HALF, rows - HALF, rows).astype(f32) * step
    wave_columns = jnp.where(columns > HALF, columns - HALF, columns).astype(f32) * step
    plane_square = wave_rows * wave_rows + wave_columns * wave_columns
    first_line = lax.axis_index("gy") * lax.axis_size("gz") + lax.axis_index("gz")
    filtered = []
    for part in range(2):
        spectrum = dot3(forward, split(depth[part * N : (part + 1) * N]), NN)
        line = first_line + (HALF if part == 1 else 0) * (first_line == 0).astype(jnp.int32)
        wave_line = line.astype(f32) * step
        square = plane_square + wave_line * wave_line
        filtered.append(
            jnp.where(square > 0.0, spectrum / jnp.where(square > 0.0, square, 1.0), 0.0)
        )
    stacked = split(jnp.concatenate(filtered, axis=0))
    plain = split(dot3(stacked, inverse, NN))
    sloped = split(dot3(stacked, slope, NN))
    part_of = lambda pair, part: tuple(v[part * N : (part + 1) * N] for v in pair)
    for field, (matrix, values) in enumerate(
        ((inverse_t, plain), (slope_t, plain), (inverse_t, sloped))
    ):
        first = dot3(matrix, part_of(values, 0), NN)
        second = dot3(matrix, part_of(values, 1), NN)
        for g in (0, 2):
            lanes = slice(g * DEPTH, g * DEPTH + 128)
            a, b = first[:, lanes], second[:, lanes]
            even = jnp.where(mask, a, pltpu.roll(b, DEPTH, 1))
            odd = jnp.where(mask, pltpu.roll(a, DEPTH, 1), b)
            out_ref[:, g, field * ROWS : (field + 1) * ROWS, :] = even.reshape(32, ROWS, 128)
            out_ref[:, g + 1, field * ROWS : (field + 1) * ROWS, :] = odd.reshape(32, ROWS, 128)


def planes(values):
    whole = pl.BlockSpec(memory_space=pltpu.VMEM)
    tables = [
        jnp.asarray(split_table(t))
        for t in (forward_table, inverse_table, slope_table, inverse_table.T, slope_table.T)
    ]
    return pl.pallas_call(
        planes_kernel,
        in_specs=[whole] * 6,
        out_specs=whole,
        out_shape=jax.ShapeDtypeStruct((32, 4, 3 * ROWS, 128), f32),
        compiler_params=pltpu.CompilerParams(vmem_limit_bytes=24 << 20),
        name="planes",
    )(values, *tables)


PAD = 8
HELD = DEPTH + 2 * PAD
EDGE_ROWS = (0, 1, ROWS - 2, ROWS - 1)
EVERY_ROW = tuple(range(ROWS))


def tile_weights(moved):
    weights = []
    for shift in range(5):
        offset = moved + (shift - 2.0) if shift != 2 else moved
        outer = jnp.maximum(2.0 - jnp.abs(offset), 0.0)
        weights.append(
            jnp.minimum(4.0 - 3.0 * ((offset * offset) * outer), (outer * outer) * outer)
        )
    return weights


def row_pair(row, slots, in_ref, displacement_ref, inverse, slope, psi_ref, weight_ref):
    mask = low_lanes((HALF, 128))
    for field in range(3):
        start = field * ROWS + row
        even = in_ref[pl.ds(start, HALF, stride=3 * ROWS), :]
        odd = in_ref[pl.ds(start + 1, HALF, stride=3 * ROWS), :]
        first = jnp.where(mask, even, pltpu.roll(odd, DEPTH, 1))
        second = jnp.where(mask, pltpu.roll(even, DEPTH, 1), odd)
        stacked = jnp.concatenate([first, second], axis=0)
        result = dot3(split(stacked), slope if field == 0 else inverse, TN)
        for part, slot in enumerate(slots):
            values = result[part * DEPTH : (part + 1) * DEPTH]
            psi_ref[slot, field] = values
            for tile in range(DEPTH // 8):
                for half in range(2):
                    lanes = slice(half * 128, half * 128 + 128)
                    rows = slice(tile * 8, tile * 8 + 8)
                    moved = displacement_ref[field, row + part, rows, lanes] + values[rows, lanes]
                    for shift, weight in enumerate(tile_weights(moved)):
                        weight_ref[slot, 5 * field + shift, half, rows, :] = weight


def shift_lines(halves):
    lane = lax.broadcasted_iota(jnp.int32, (8, 128), 1)
    low, high = halves[0][2], halves[1][2]
    for shift_line in (0, 1, 3, 4):
        move = 2 - shift_line
        a = pltpu.roll(halves[0][shift_line], move % 128, 1)
        b = pltpu.roll(halves[1][shift_line], move % 128, 1)
        wraps = lane < move if move > 0 else lane >= 128 + move
        low = low + jnp.where(wraps, b, a)
        high = high + jnp.where(wraps, a, b)
    return low * (1.0 / 216.0), high * (1.0 / 216.0)


def add_up(terms):
    while len(terms) > 1:
        terms = [sum(terms[i : i + 2][1:], terms[i]) for i in range(0, len(terms), 2)]
    return terms[0]


def collect(sum_ref, jobs):
    for half in range(2):
        for shift_depth in range(5):
            for shift_line in range(5):
                zeros = jnp.zeros((PAD, 128), f32)
                sum_ref[half, shift_depth, shift_line, 0:PAD, :] = zeros
                sum_ref[half, shift_depth, shift_line, HELD - PAD : HELD, :] = zeros

    for pairs, out_ref, row in jobs:

        @pl.loop(0, DEPTH // 8)
        def _(tile):
            start = pl.multiple_of(tile * 8, 8)
            for half in range(2):
                totals = None
                for (weight_ref, slot), shift_row in pairs:
                    get = lambda i: weight_ref[slot, i, half, pl.ds(start, 8), :]
                    line_weights = [get(i) for i in range(5)]
                    row_weight = get(5 + shift_row)
                    planes = [row_weight * get(10 + d) for d in range(5)]
                    terms = [[plane * w for w in line_weights] for plane in planes]
                    totals = (
                        terms
                        if totals is None
                        else [[a + b for a, b in zip(x, y)] for x, y in zip(totals, terms)]
                    )
                for d in range(5):
                    for shift_line in range(5):
                        value = totals[d][shift_line]
                        sum_ref[half, d, shift_line, pl.ds(start + PAD, 8), :] = value

        for tile in range(DEPTH // 8 + 1):
            if tile < DEPTH // 8:
                places = [(d, tile * 8 + PAD - 2 + d) for d in range(5)]
            else:
                places = [(d, PAD + DEPTH - 2 + d) for d in (0, 1)]
                places += [(d, d - 2) for d in (3, 4)]
            halves = [
                [
                    add_up([sum_ref[half, d, shift_line, at : at + 8, :] for d, at in places])
                    for shift_line in range(5)
                ]
                for half in range(2)
            ]
            low, high = shift_lines(halves)
            out_ref[row, tile * 8 : tile * 8 + 8, 0:128] = low
            out_ref[row, tile * 8 : tile * 8 + 8, 128:256] = high


def reach(cell, held):
    return [(held[row], row + 2 - cell) for row in sorted(held) if 0 <= row + 2 - cell < 5]


def edges_kernel(
    in_ref, displacement_ref, inverse_ref, slope_ref,
    psi_out, weight_ref, first_ref, second_ref,
    psi_ref, sum_ref, psi_sem,
):
    inverse = (inverse_ref[0], inverse_ref[1])
    slope = (slope_ref[0], slope_ref[1])
    copies = []
    for pair, row in enumerate((0, ROWS - 2)):
        slots = (2 * pair, 2 * pair + 1)
        row_pair(row, slots, in_ref, displacement_ref, inverse, slope, psi_ref, weight_ref)
        for part, slot in enumerate(slots):
            copy = pltpu.make_async_copy(
                psi_ref.at[slot], psi_out.at[:, row + part], psi_sem.at[slot]
            )
            copy.start()
            copies.append(copy)
    held = {row: (weight_ref, slot) for slot, row in enumerate(EDGE_ROWS)}

    def cells(before_ref, after_ref):
        jobs = [(reach(index - 2, held), before_ref, index) for index in range(2)]
        jobs += [(reach(ROWS + index, held), after_ref, index) for index in range(2)]
        collect(sum_ref, jobs)

    odd = lax.axis_index("gy") % 2

    @pl.when(odd == 0)
    def _():
        cells(second_ref, first_ref)

    @pl.when(odd != 0)
    def _():
        cells(first_ref, second_ref)

    for copy in copies:
        copy.wait()


VMEM = pl.BlockSpec(memory_space=pltpu.VMEM)
SMEM = pl.BlockSpec(memory_space=pltpu.SMEM)
ANY = pl.BlockSpec(memory_space=pl.ANY)


def edges(values, displacement, tables):
    halo = jax.ShapeDtypeStruct((2, DEPTH + PAD, N), f32)
    return pl.pallas_call(
        edges_kernel,
        in_specs=[VMEM] * 4,
        out_specs=[ANY, VMEM, VMEM, VMEM],
        out_shape=[
            jax.ShapeDtypeStruct((3, ROWS, DEPTH, N), f32),
            jax.ShapeDtypeStruct((4, 15, 2, DEPTH + PAD, 128), f32),
            halo,
            halo,
        ],
        scratch_shapes=[
            pltpu.VMEM((4, 3, DEPTH, N), f32),
            pltpu.VMEM((2, 5, 5, HELD + PAD, 128), f32),
            pltpu.SemaphoreType.DMA((4,)),
        ],
        compiler_params=pltpu.CompilerParams(vmem_limit_bytes=16 << 20),
        name="edges",
    )(values, displacement, *tables)


def inner_kernel(
    in_ref, displacement_ref, inverse_ref, slope_ref, psi_in, edge_ref,
    psi_out, out_ref,
    psi_ref, weight_ref, sum_ref, psi_sem,
):
    inverse = (inverse_ref[0], inverse_ref[1])
    slope = (slope_ref[0], slope_ref[1])
    copies = []
    for row in (2, 4):
        slots = (row - 2, row - 1)
        row_pair(row, slots, in_ref, displacement_ref, inverse, slope, psi_ref, weight_ref)
        for slot in slots:
            copy = pltpu.make_async_copy(
                psi_ref.at[slot], psi_out.at[:, slot + 2], psi_sem.at[slot]
            )
            copy.start()
            copies.append(copy)
    held = {row: (edge_ref, slot) for slot, row in enumerate(EDGE_ROWS)}
    held.update({row: (weight_ref, row - 2) for row in range(2, ROWS - 2)})
    collect(sum_ref, [(reach(row, held), out_ref, row) for row in range(ROWS)])
    for copy in copies:
        copy.wait()


def inner(values, displacement, tables, psi, weights):
    return pl.pallas_call(
        inner_kernel,
        in_specs=[VMEM] * 4 + [ANY, VMEM],
        out_specs=[ANY, VMEM],
        out_shape=[
            jax.ShapeDtypeStruct((3, ROWS, DEPTH, N), f32),
            jax.ShapeDtypeStruct((ROWS, DEPTH + PAD, N), f32),
        ],
        scratch_shapes=[
            pltpu.VMEM((4, 3, DEPTH, N), f32),
            pltpu.VMEM((4, 15, 2, DEPTH + PAD, 128), f32),
            pltpu.VMEM((2, 5, 5, HELD + PAD, 128), f32),
            pltpu.SemaphoreType.DMA((4,)),
        ],
        input_output_aliases={4: 0},
        compiler_params=pltpu.CompilerParams(vmem_limit_bytes=20 << 20),
        name="inner",
    )(values, displacement, *tables, psi, weights)


def halos(first_ref, second_ref, where):
    even = lax.axis_index("gy") % 2 == 0
    first, second = first_ref[:, where, :], second_ref[:, where, :]
    return jnp.where(even, second, first), jnp.where(even, first, second)


def sides_kernel(cell_ref, first_ref, second_ref, out_ref):
    low, high = halos(first_ref, second_ref, slice(None))
    side = cell_ref[...]
    out_ref[0:2] = side[0:2] + low
    out_ref[2 : ROWS - 2] = side[2 : ROWS - 2]
    out_ref[ROWS - 2 :] = side[ROWS - 2 :] + high


def sides(cells, first, second):
    last = DEPTH // PAD
    block = lambda rows: pl.BlockSpec((rows, PAD, N), lambda i: (0, last, 0))
    return pl.pallas_call(
        sides_kernel,
        grid=(1,),
        in_specs=[block(ROWS), block(2), block(2)],
        out_specs=pl.BlockSpec((ROWS, PAD, N), lambda i: (0, 0, 0)),
        out_shape=jax.ShapeDtypeStruct((ROWS, PAD, N), f32),
        compiler_params=pltpu.CompilerParams(vmem_limit_bytes=8 << 20),
        name="sides",
    )(cells, first, second)


def sum_kernel(cell_ref, first_ref, second_ref, left_ref, right_ref, out_ref):
    low, high = halos(first_ref, second_ref, slice(0, DEPTH))
    sub = lax.broadcasted_iota(jnp.int32, (PAD, N), 0)
    for row in range(ROWS):
        value = cell_ref[row, :DEPTH, :] - 1.0
        if row < 2:
            value = value + low[row]
        if row >= ROWS - 2:
            value = value + high[row - ROWS + 2]
        out_ref[row, 0:8, :] = value[0:8] + jnp.where(sub < 2, left_ref[row], 0.0)
        out_ref[row, 8:56, :] = value[8:56]
        out_ref[row, 56:64, :] = value[56:64] + jnp.where(sub >= 6, right_ref[row], 0.0)


def total(*parts):
    return pl.pallas_call(
        sum_kernel,
        in_specs=[VMEM] * 5,
        out_specs=VMEM,
        out_shape=jax.ShapeDtypeStruct((ROWS, DEPTH, N), f32),
        compiler_params=pltpu.CompilerParams(vmem_limit_bytes=8 << 20),
        name="total",
    )(*parts)


def local(hessian_one, hessian_two, displacement):
    size_y, size_z = lax.axis_size("gy"), lax.axis_size("gz")
    both = ("gy", "gz")
    spectra = lines(hessian_one, hessian_two).reshape(HALF, ROWS, 128)
    spectra = lax.all_to_all(spectra, both, split_axis=0, concat_axis=0, tiled=True)
    returned = planes(spectra.reshape(32, 4, ROWS, 128))
    returned = returned.reshape(HALF, 3 * ROWS, 128)
    returned = lax.all_to_all(returned, both, split_axis=0, concat_axis=0, tiled=True)
    returned = returned.reshape(HALF * 3 * ROWS, 128)
    tables = [jnp.asarray(split_table(t)) for t in (inverse_table, slope_table)]
    psi, weights, first, second = edges(returned, displacement, tables)
    first = lax.ppermute(first, "gy", [(i, i ^ 1) for i in range(size_y)])
    second = lax.ppermute(
        second, "gy", [(i, (i + (1 if i % 2 else -1)) % size_y) for i in range(size_y)]
    )
    psi, cells = inner(returned, displacement, tables, psi, weights)
    side = sides(cells, first, second)
    up = [(i, (i + 1) % size_z) for i in range(size_z)]
    down = [(j, i) for i, j in up]
    left = lax.ppermute(side, "gz", up)
    right = lax.ppermute(side, "gz", down)
    density = total(cells, first, second, left, right)
    return psi, density


def solution(mesh):
    in_specs = (P(None, "gy", "gz", None), P(None, "gy", "gz", None), P(None, "gy", "gz", None))
    out_specs = (P(None, "gy", "gz", None), P("gy", "gz", None))
    return jax.shard_map(local, mesh=mesh, in_specs=in_specs, out_specs=out_specs, check_vma=False)
```

```python
import functools

import jax
import jax.numpy as jnp
import numpy as np
from jax import lax
from jax.experimental import pallas as pl
from jax.experimental.pallas import tpu as pltpu
from jax.sharding import PartitionSpec as P

N = 256
HALF = N // 2
ROWS = 8
DEPTH = 64
det_weight = -1.0 / 3.0
mixed_weight = 10.0 / 21.0
f32 = jnp.float32
bf16 = jnp.bfloat16


def split_table(table):
    high = table.astype(np.float32).astype(jnp.bfloat16)
    low = (table - high.astype(np.float64)).astype(np.float32).astype(jnp.bfloat16)
    return np.stack([high, low])


def wave_index():
    order = np.arange(N)
    return np.where(order <= HALF, order, order - HALF)


def real_tables():
    order = np.arange(N)
    wave = wave_index()
    is_sin = order > HALF
    angle = 2.0 * np.pi / N * (wave[:, None] * np.arange(N)[None, :] % N)
    cosine, sine = np.cos(angle), np.sin(angle)
    forward = np.where(is_sin[:, None], sine, cosine)
    single = (order == 0) | (order == HALF)
    weight = np.where(single, 1.0, 2.0)[:, None] / N
    inverse = weight * forward
    number = (2.0 * np.pi / N * np.where(single, 0, wave))[:, None]
    slope = weight * number * np.where(is_sin[:, None], cosine, -sine)
    return forward, inverse, slope


forward_table, inverse_table, slope_table = real_tables()


def split(value):
    high = value.astype(bf16)
    return high, (value - high.astype(f32)).astype(bf16)


def dot3(left, right, dims):
    (left_high, left_low), (right_high, right_low) = left, right
    product = functools.partial(
        lax.dot_general, dimension_numbers=(dims, ((), ())), preferred_element_type=f32
    )
    return product(left_high, right_high) + (
        product(left_high, right_low) + product(left_low, right_high)
    )


NN = ((1,), (0,))
NT = ((1,), (1,))
TN = ((0,), (0,))


def low_lanes(shape):
    return lax.broadcasted_iota(jnp.int32, shape, len(shape) - 1) < DEPTH


def source_term(one, two):
    primary = [one[c].astype(f32) for c in range(6)]
    secondary = [two[c].astype(f32) for c in range(6)]
    determinant = (
        primary[0] * (primary[1] * primary[2] - primary[5] * primary[5])
        - primary[3] * (primary[3] * primary[2] - primary[5] * primary[4])
        + primary[4] * (primary[3] * primary[5] - primary[1] * primary[4])
    )
    mixed = 0.5 * (
        secondary[0] * (primary[1] + primary[2])
        + secondary[1] * (primary[0] + primary[2])
        + secondary[2] * (primary[0] + primary[1])
    )
    mixed = mixed - (
        secondary[3] * primary[3] + secondary[4] * primary[4] + secondary[5] * primary[5]
    )
    return det_weight * determinant + mixed_weight * mixed


def lines_kernel(one_in, two_in, table_in, out_ref, one_ref, two_ref, table_ref, sem):
    table_copy = pltpu.make_async_copy(table_in, table_ref, sem.at[ROWS])
    table_copy.start()
    copies = []
    for pair in range(ROWS // 2):
        rows = slice(2 * pair, 2 * pair + 2)
        for index, (source, target) in enumerate(((one_in, one_ref), (two_in, two_ref))):
            copy = pltpu.make_async_copy(
                source.at[:, rows], target.at[:, rows], sem.at[2 * pair + index]
            )
            copy.start()
            copies.append(copy)
    mask = low_lanes((HALF, 128))
    table_copy.wait()
    for pair in range(ROWS // 2):
        copies[2 * pair].wait()
        copies[2 * pair + 1].wait()
        source = jnp.concatenate(
            [
                source_term(
                    [one_ref[c, row] for c in range(6)], [two_ref[c, row] for c in range(6)]
                )
                for row in (2 * pair, 2 * pair + 1)
            ],
            axis=0,
        )
        result = dot3((table_ref[0], table_ref[1]), split(source), NT)
        first, second = result[:HALF], result[HALF:]
        out_ref[pl.ds(2 * pair, HALF, stride=ROWS), :] = jnp.where(
            mask, first, pltpu.roll(second, DEPTH, 1)
        )
        out_ref[pl.ds(2 * pair + 1, HALF, stride=ROWS), :] = jnp.where(
            mask, pltpu.roll(first, DEPTH, 1), second
        )


def lines(one, two):
    far = pl.BlockSpec(memory_space=pltpu.HBM)
    return pl.pallas_call(
        lines_kernel,
        in_specs=[far] * 3,
        out_specs=pl.BlockSpec(memory_space=pltpu.VMEM),
        out_shape=jax.ShapeDtypeStruct((HALF * ROWS, 128), f32),
        scratch_shapes=[
            pltpu.VMEM((6, ROWS, DEPTH, N), bf16),
            pltpu.VMEM((6, ROWS, DEPTH, N), bf16),
            pltpu.VMEM((2, N, N), bf16),
            pltpu.SemaphoreType.DMA((ROWS + 1,)),
        ],
        compiler_params=pltpu.CompilerParams(vmem_limit_bytes=16 << 20),
        name="lines",
    )(
        pltpu.with_memory_space_constraint(one, pltpu.HBM),
        pltpu.with_memory_space_constraint(two, pltpu.HBM),
        pltpu.with_memory_space_constraint(jnp.asarray(split_table(forward_table)), pltpu.HBM),
    )


def planes_kernel(in_ref, forward_ref, inverse_ref, slope_ref, inverse_t_ref, slope_t_ref, out_ref):
    mask = low_lanes((N, 128))
    tiles = [in_ref[:, g].reshape(N, 128) for g in range(4)]
    swapped = [pltpu.roll(tile, DEPTH, 1) for tile in tiles]
    first = [jnp.where(mask, tiles[g], swapped[g + 1]) for g in (0, 2)]
    second = [jnp.where(mask, swapped[g], tiles[g + 1]) for g in (0, 2)]
    stacked = jnp.concatenate(
        [jnp.concatenate(first, axis=1), jnp.concatenate(second, axis=1)], axis=0
    )
    forward = (forward_ref[0], forward_ref[1])
    inverse = (inverse_ref[0], inverse_ref[1])
    slope = (slope_ref[0], slope_ref[1])
    inverse_t = (inverse_t_ref[0], inverse_t_ref[1])
    slope_t = (slope_t_ref[0], slope_t_ref[1])
    depth = dot3(split(stacked), forward, NT)
    step = 2.0 * np.pi / N
    rows = lax.broadcasted_iota(jnp.int32, (N, N), 0)
    columns = lax.broadcasted_iota(jnp.int32, (N, N), 1)
    wave_rows = jnp.where(rows > HALF, rows - HALF, rows).astype(f32) * step
    wave_columns = jnp.where(columns > HALF, columns - HALF, columns).astype(f32) * step
    plane_square = wave_rows * wave_rows + wave_columns * wave_columns
    first_line = lax.axis_index("gy") * lax.axis_size("gz") + lax.axis_index("gz")
    filtered = []
    for part in range(2):
        spectrum = dot3(forward, split(depth[part * N : (part + 1) * N]), NN)
        line = first_line + (HALF if part == 1 else 0) * (first_line == 0).astype(jnp.int32)
        wave_line = line.astype(f32) * step
        square = plane_square + wave_line * wave_line
        filtered.append(
            jnp.where(square > 0.0, spectrum / jnp.where(square > 0.0, square, 1.0), 0.0)
        )
    stacked = split(jnp.concatenate(filtered, axis=0))
    plain = split(dot3(stacked, inverse, NN))
    sloped = split(dot3(stacked, slope, NN))
    part_of = lambda pair, part: tuple(v[part * N : (part + 1) * N] for v in pair)
    for field, (matrix, values) in enumerate(
        ((inverse_t, plain), (slope_t, plain), (inverse_t, sloped))
    ):
        first = dot3(matrix, part_of(values, 0), NN)
        second = dot3(matrix, part_of(values, 1), NN)
        for g in (0, 2):
            lanes = slice(g * DEPTH, g * DEPTH + 128)
            a, b = first[:, lanes], second[:, lanes]
            even = jnp.where(mask, a, pltpu.roll(b, DEPTH, 1))
            odd = jnp.where(mask, pltpu.roll(a, DEPTH, 1), b)
            out_ref[:, g, field * ROWS : (field + 1) * ROWS, :] = even.reshape(32, ROWS, 128)
            out_ref[:, g + 1, field * ROWS : (field + 1) * ROWS, :] = odd.reshape(32, ROWS, 128)


def planes(values, tables):
    whole = pl.BlockSpec(memory_space=pltpu.VMEM)
    return pl.pallas_call(
        planes_kernel,
        in_specs=[whole] * 6,
        out_specs=whole,
        out_shape=jax.ShapeDtypeStruct((32, 4, 3 * ROWS, 128), f32),
        compiler_params=pltpu.CompilerParams(vmem_limit_bytes=24 << 20),
        name="planes",
    )(values, *tables)


PAD = 8
HELD = DEPTH + 2 * PAD
EDGE_ROWS = (0, 1, ROWS - 2, ROWS - 1)
EVERY_ROW = tuple(range(ROWS))


def tile_weights(moved):
    cell = jnp.floor(moved)
    rise = moved - cell
    fall = 1.0 - rise
    rise2, fall2 = rise * rise, fall * fall
    outer_low, outer_high = rise2 * rise, fall2 * fall
    inner_high = 4.0 - 3.0 * (rise2 * (1.0 + fall))
    inner_low = 4.0 - 3.0 * (fall2 * (1.0 + rise))
    pieces = (outer_low, inner_low, inner_high, outer_high)
    at = {n: cell == n for n in range(-4, 4)}
    weights = []
    for offset in range(-2, 3):
        weight = jnp.zeros_like(moved)
        for piece, value in zip(range(-2, 2), pieces):
            weight = jnp.where(at[piece - offset], value, weight)
        weights.append(weight)
    return weights


def row_pair(row, slots, in_ref, displacement_ref, inverse, slope, psi_ref, weight_ref):
    mask = low_lanes((HALF, 128))
    for field in range(3):
        start = field * ROWS + row
        even = in_ref[pl.ds(start, HALF, stride=3 * ROWS), :]
        odd = in_ref[pl.ds(start + 1, HALF, stride=3 * ROWS), :]
        first = jnp.where(mask, even, pltpu.roll(odd, DEPTH, 1))
        second = jnp.where(mask, pltpu.roll(even, DEPTH, 1), odd)
        stacked = jnp.concatenate([first, second], axis=0)
        result = dot3(split(stacked), slope if field == 0 else inverse, TN)
        for part, slot in enumerate(slots):
            values = result[part * DEPTH : (part + 1) * DEPTH]
            psi_ref[slot, field] = values
            for tile in range(DEPTH // 8):
                for half in range(2):
                    lanes = slice(half * 128, half * 128 + 128)
                    rows = slice(tile * 8, tile * 8 + 8)
                    moved = displacement_ref[field, row + part, rows, lanes] + values[rows, lanes]
                    for shift, weight in enumerate(tile_weights(moved)):
                        weight_ref[slot, 5 * field + shift, half, rows, :] = weight


def shift_lines(halves):
    lane = lax.broadcasted_iota(jnp.int32, (8, 128), 1)
    low, high = halves[0][2], halves[1][2]
    for shift_line in (0, 1, 3, 4):
        move = 2 - shift_line
        a = pltpu.roll(halves[0][shift_line], move % 128, 1)
        b = pltpu.roll(halves[1][shift_line], move % 128, 1)
        wraps = lane < move if move > 0 else lane >= 128 + move
        low = low + jnp.where(wraps, b, a)
        high = high + jnp.where(wraps, a, b)
    return low * (1.0 / 216.0), high * (1.0 / 216.0)


def add_up(terms):
    while len(terms) > 1:
        terms = [sum(terms[i : i + 2][1:], terms[i]) for i in range(0, len(terms), 2)]
    return terms[0]


def collect(sum_ref, jobs):
    for half in range(2):
        for shift_depth in range(5):
            for shift_line in range(5):
                zeros = jnp.zeros((PAD, 128), f32)
                sum_ref[half, shift_depth, shift_line, 0:PAD, :] = zeros
                sum_ref[half, shift_depth, shift_line, HELD - PAD : HELD, :] = zeros

    for pairs, out_ref, row in jobs:

        @pl.loop(0, DEPTH // 8)
        def _(tile):
            start = pl.multiple_of(tile * 8, 8)
            for half in range(2):
                totals = None
                for (weight_ref, slot), shift_row in pairs:
                    get = lambda i: weight_ref[slot, i, half, pl.ds(start, 8), :]
                    line_weights = [get(i) for i in range(5)]
                    row_weight = get(5 + shift_row)
                    planes = [row_weight * get(10 + d) for d in range(5)]
                    terms = [[plane * w for w in line_weights] for plane in planes]
                    totals = (
                        terms
                        if totals is None
                        else [[a + b for a, b in zip(x, y)] for x, y in zip(totals, terms)]
                    )
                for d in range(5):
                    for shift_line in range(5):
                        value = totals[d][shift_line]
                        sum_ref[half, d, shift_line, pl.ds(start + PAD, 8), :] = value

        for tile in range(DEPTH // 8 + 1):
            if tile < DEPTH // 8:
                places = [(d, tile * 8 + PAD - 2 + d) for d in range(5)]
            else:
                places = [(d, PAD + DEPTH - 2 + d) for d in (0, 1)]
                places += [(d, d - 2) for d in (3, 4)]
            halves = [
                [
                    add_up([sum_ref[half, d, shift_line, at : at + 8, :] for d, at in places])
                    for shift_line in range(5)
                ]
                for half in range(2)
            ]
            low, high = shift_lines(halves)
            out_ref[row, tile * 8 : tile * 8 + 8, 0:128] = low
            out_ref[row, tile * 8 : tile * 8 + 8, 128:256] = high


def reach(cell, held):
    return [(held[row], row + 2 - cell) for row in sorted(held) if 0 <= row + 2 - cell < 5]


def edges_kernel(
    in_ref, displacement_ref, inverse_ref, slope_ref,
    psi_out, weight_ref, second_ref, first_ref,
    psi_ref, sum_ref, psi_sem,
):
    inverse = (inverse_ref[0], inverse_ref[1])
    slope = (slope_ref[0], slope_ref[1])
    copies = []
    for pair, row in enumerate((0, ROWS - 2)):
        slots = (2 * pair, 2 * pair + 1)
        row_pair(row, slots, in_ref, displacement_ref, inverse, slope, psi_ref, weight_ref)
        for part, slot in enumerate(slots):
            copy = pltpu.make_async_copy(
                psi_ref.at[slot], psi_out.at[:, row + part], psi_sem.at[slot]
            )
            copy.start()
            copies.append(copy)
    held = {row: (weight_ref, slot) for slot, row in enumerate(EDGE_ROWS)}

    def cells(before_ref, after_ref):
        jobs = [(reach(index - 2, held), before_ref, index) for index in range(2)]
        jobs += [(reach(ROWS + index, held), after_ref, index) for index in range(2)]
        collect(sum_ref, jobs)

    odd = lax.axis_index("gy") % 2

    @pl.when(odd == 0)
    def _():
        cells(second_ref, first_ref)

    @pl.when(odd != 0)
    def _():
        cells(first_ref, second_ref)

    for copy in copies:
        copy.wait()


VMEM = pl.BlockSpec(memory_space=pltpu.VMEM)
SMEM = pl.BlockSpec(memory_space=pltpu.SMEM)
ANY = pl.BlockSpec(memory_space=pl.ANY)


def edges(values, displacement, tables):
    halo = jax.ShapeDtypeStruct((2, DEPTH + PAD, N), f32)
    return pl.pallas_call(
        edges_kernel,
        in_specs=[VMEM] * 4,
        out_specs=[ANY, VMEM, VMEM, VMEM],
        out_shape=[
            jax.ShapeDtypeStruct((3, ROWS, DEPTH, N), f32),
            jax.ShapeDtypeStruct((4, 15, 2, DEPTH + PAD, 128), f32),
            halo,
            halo,
        ],
        scratch_shapes=[
            pltpu.VMEM((4, 3, DEPTH, N), f32),
            pltpu.VMEM((2, 5, 5, HELD + PAD, 128), f32),
            pltpu.SemaphoreType.DMA((4,)),
        ],
        compiler_params=pltpu.CompilerParams(vmem_limit_bytes=16 << 20),
        name="edges",
    )(values, displacement, *tables)


def inner_kernel(
    in_ref, displacement_ref, inverse_ref, slope_ref, psi_in, edge_ref,
    psi_out, out_ref,
    psi_ref, weight_ref, sum_ref, psi_sem,
):
    inverse = (inverse_ref[0], inverse_ref[1])
    slope = (slope_ref[0], slope_ref[1])
    copies = []
    for row in (2, 4):
        slots = (row - 2, row - 1)
        row_pair(row, slots, in_ref, displacement_ref, inverse, slope, psi_ref, weight_ref)
        for slot in slots:
            copy = pltpu.make_async_copy(
                psi_ref.at[slot], psi_out.at[:, slot + 2], psi_sem.at[slot]
            )
            copy.start()
            copies.append(copy)
    held = {row: (edge_ref, slot) for slot, row in enumerate(EDGE_ROWS)}
    held.update({row: (weight_ref, row - 2) for row in range(2, ROWS - 2)})
    collect(sum_ref, [(reach(row, held), out_ref, row) for row in range(ROWS)])
    for copy in copies:
        copy.wait()


def inner(values, displacement, tables, psi, weights):
    return pl.pallas_call(
        inner_kernel,
        in_specs=[VMEM] * 4 + [ANY, VMEM],
        out_specs=[ANY, VMEM],
        out_shape=[
            jax.ShapeDtypeStruct((3, ROWS, DEPTH, N), f32),
            jax.ShapeDtypeStruct((ROWS, DEPTH + PAD, N), f32),
        ],
        scratch_shapes=[
            pltpu.VMEM((4, 3, DEPTH, N), f32),
            pltpu.VMEM((4, 15, 2, DEPTH + PAD, 128), f32),
            pltpu.VMEM((2, 5, 5, HELD + PAD, 128), f32),
            pltpu.SemaphoreType.DMA((4,)),
        ],
        input_output_aliases={4: 0},
        compiler_params=pltpu.CompilerParams(vmem_limit_bytes=20 << 20),
        name="inner",
    )(values, displacement, *tables, psi, weights)


def ordered(axis, first, second):
    even = lax.axis_index(axis) % 2 == 0
    return jnp.where(even, second, first), jnp.where(even, first, second)


def sides_kernel(cell_ref, first_ref, second_ref, low_ref, high_ref):
    low, high = ordered("gy", first_ref[...], second_ref[...])
    side = cell_ref[...]
    side = jnp.concatenate(
        [side[0:2] + low, side[2 : ROWS - 2], side[ROWS - 2 :] + high], axis=0
    )
    above, below = side[:, 0:2, :], side[:, PAD - 2 :, :]
    even = lax.axis_index("gz") % 2 == 0
    low_ref[...] = jnp.where(even, above, below)
    high_ref[...] = jnp.where(even, below, above)


def sides(cells, first, second):
    last = DEPTH // PAD
    block = lambda rows: pl.BlockSpec((rows, PAD, N), lambda i: (0, last, 0))
    side = jax.ShapeDtypeStruct((ROWS, 2, N), f32)
    return pl.pallas_call(
        sides_kernel,
        grid=(1,),
        in_specs=[block(ROWS), block(2), block(2)],
        out_specs=[pl.BlockSpec((ROWS, 2, N), lambda i: (0, 0, 0))] * 2,
        out_shape=[side, side],
        compiler_params=pltpu.CompilerParams(vmem_limit_bytes=8 << 20),
        name="sides",
    )(cells, first, second)


def sum_kernel(cell_ref, first_ref, second_ref, near_ref, far_ref, out_ref):
    low, high = ordered("gy", first_ref[:, :DEPTH, :], second_ref[:, :DEPTH, :])
    left, right = ordered("gz", near_ref[...], far_ref[...])
    for row in range(ROWS):
        value = cell_ref[row, :DEPTH, :] - 1.0
        if row < 2:
            value = value + low[row]
        if row >= ROWS - 2:
            value = value + high[row - ROWS + 2]
        out_ref[row, 0:2, :] = value[0:2] + left[row]
        out_ref[row, 2:8, :] = value[2:8]
        out_ref[row, 8:56, :] = value[8:56]
        out_ref[row, 56:62, :] = value[56:62]
        out_ref[row, 62:64, :] = value[62:64] + right[row]


def total(*parts):
    return pl.pallas_call(
        sum_kernel,
        in_specs=[VMEM] * 5,
        out_specs=VMEM,
        out_shape=jax.ShapeDtypeStruct((ROWS, DEPTH, N), f32),
        compiler_params=pltpu.CompilerParams(vmem_limit_bytes=8 << 20),
        name="total",
    )(*parts)


def swap(value, axis, rounds):
    size = lax.axis_size(axis)
    return lax.ppermute(
        value, axis, [(i, (i + (1 if i % 2 == rounds else -1)) % size) for i in range(size)]
    )


def local(hessian_one, hessian_two, displacement):
    both = ("gy", "gz")
    tables = [
        jnp.asarray(split_table(t))
        for t in (forward_table, inverse_table, slope_table, inverse_table.T, slope_table.T)
    ]
    spectra = lines(hessian_one, hessian_two)
    spectra = spectra.reshape(HALF, ROWS, 128)
    spectra = lax.all_to_all(spectra, both, split_axis=0, concat_axis=0, tiled=True)
    returned = planes(spectra.reshape(32, 4, ROWS, 128), tables)
    returned = returned.reshape(HALF, 3 * ROWS, 128)
    returned = lax.all_to_all(returned, both, split_axis=0, concat_axis=0, tiled=True)
    returned = returned.reshape(HALF * 3 * ROWS, 128)
    tables = tables[1:3]
    psi, weights, second, first = edges(returned, displacement, tables)
    second = swap(second, "gy", 1)
    first = swap(first, "gy", 0)
    psi, cells = inner(returned, displacement, tables, psi, weights)
    near, far = sides(cells, first, second)
    far = swap(far, "gz", 1)
    near = swap(near, "gz", 0)
    density = total(cells, first, second, near, far)
    return psi, density


def solution(mesh):
    in_specs = (P(None, "gy", "gz", None), P(None, "gy", "gz", None), P(None, "gy", "gz", None))
    out_specs = (P(None, "gy", "gz", None), P("gy", "gz", None))
    return jax.shard_map(local, mesh=mesh, in_specs=in_specs, out_specs=out_specs, check_vma=False)
```

```python
import functools

import jax
import jax.numpy as jnp
import numpy as np
from jax import lax
from jax.experimental import pallas as pl
from jax.experimental.pallas import tpu as pltpu
from jax.sharding import PartitionSpec as P


N = 256
HALF = N // 2
ROWS = 8
DEPTH = 64
det_weight = -1.0 / 3.0
mixed_weight = 10.0 / 21.0
f32 = jnp.float32
bf16 = jnp.bfloat16


def split_table(table):
    high = table.astype(np.float32).astype(jnp.bfloat16)
    low = (table - high.astype(np.float64)).astype(np.float32).astype(jnp.bfloat16)
    return np.stack([high, low])


def wave_index():
    order = np.arange(N)
    return np.where(order <= HALF, order, order - HALF)


def real_tables():
    order = np.arange(N)
    wave = wave_index()
    is_sin = order > HALF
    angle = 2.0 * np.pi / N * (wave[:, None] * np.arange(N)[None, :] % N)
    cosine, sine = np.cos(angle), np.sin(angle)
    forward = np.where(is_sin[:, None], sine, cosine)
    single = (order == 0) | (order == HALF)
    weight = np.where(single, 1.0, 2.0)[:, None] / N
    inverse = weight * forward
    number = (2.0 * np.pi / N * np.where(single, 0, wave))[:, None]
    slope = weight * number * np.where(is_sin[:, None], cosine, -sine)
    return forward, inverse, slope


forward_table, inverse_table, slope_table = real_tables()


def split(value):
    high = value.astype(bf16)
    return high, (value - high.astype(f32)).astype(bf16)


def dot3(left, right, dims):
    (left_high, left_low), (right_high, right_low) = left, right
    product = functools.partial(
        lax.dot_general, dimension_numbers=(dims, ((), ())), preferred_element_type=f32
    )
    return product(left_high, right_high) + (
        product(left_high, right_low) + product(left_low, right_high)
    )


NN = ((1,), (0,))
NT = ((1,), (1,))
TN = ((0,), (0,))


def low_lanes(shape):
    return lax.broadcasted_iota(jnp.int32, shape, len(shape) - 1) < DEPTH


def source_term(one, two):
    primary = [one[c].astype(f32) for c in range(6)]
    secondary = [two[c].astype(f32) for c in range(6)]
    determinant = (
        primary[0] * (primary[1] * primary[2] - primary[5] * primary[5])
        - primary[3] * (primary[3] * primary[2] - primary[5] * primary[4])
        + primary[4] * (primary[3] * primary[5] - primary[1] * primary[4])
    )
    mixed = 0.5 * (
        secondary[0] * (primary[1] + primary[2])
        + secondary[1] * (primary[0] + primary[2])
        + secondary[2] * (primary[0] + primary[1])
    )
    mixed = mixed - (
        secondary[3] * primary[3] + secondary[4] * primary[4] + secondary[5] * primary[5]
    )
    return det_weight * determinant + mixed_weight * mixed


def lines_kernel(one_in, two_in, table_in, out_ref, one_ref, two_ref, table_ref, sem):
    table_copy = pltpu.make_async_copy(table_in, table_ref, sem.at[ROWS])
    table_copy.start()
    copies = []
    for pair in range(ROWS // 2):
        rows = slice(2 * pair, 2 * pair + 2)
        for index, (source, target) in enumerate(((one_in, one_ref), (two_in, two_ref))):
            copy = pltpu.make_async_copy(
                source.at[:, rows], target.at[:, rows], sem.at[2 * pair + index]
            )
            copy.start()
            copies.append(copy)
    mask = low_lanes((HALF, 128))
    table_copy.wait()
    for pair in range(ROWS // 2):
        copies[2 * pair].wait()
        copies[2 * pair + 1].wait()
        source = jnp.concatenate(
            [
                source_term(
                    [one_ref[c, row] for c in range(6)], [two_ref[c, row] for c in range(6)]
                )
                for row in (2 * pair, 2 * pair + 1)
            ],
            axis=0,
        )
        result = dot3((table_ref[0], table_ref[1]), split(source), NT)
        first, second = result[:HALF], result[HALF:]
        out_ref[pl.ds(2 * pair, HALF, stride=ROWS), :] = jnp.where(
            mask, first, pltpu.roll(second, DEPTH, 1)
        )
        out_ref[pl.ds(2 * pair + 1, HALF, stride=ROWS), :] = jnp.where(
            mask, pltpu.roll(first, DEPTH, 1), second
        )


def lines(one, two):
    far = pl.BlockSpec(memory_space=pltpu.HBM)
    return pl.pallas_call(
        lines_kernel,
        in_specs=[far] * 3,
        out_specs=pl.BlockSpec(memory_space=pltpu.VMEM),
        out_shape=jax.ShapeDtypeStruct((HALF * ROWS, 128), f32),
        scratch_shapes=[
            pltpu.VMEM((6, ROWS, DEPTH, N), bf16),
            pltpu.VMEM((6, ROWS, DEPTH, N), bf16),
            pltpu.VMEM((2, N, N), bf16),
            pltpu.SemaphoreType.DMA((ROWS + 1,)),
        ],
        compiler_params=pltpu.CompilerParams(vmem_limit_bytes=16 << 20),
        name="lines",
    )(
        pltpu.with_memory_space_constraint(one, pltpu.HBM),
        pltpu.with_memory_space_constraint(two, pltpu.HBM),
        pltpu.with_memory_space_constraint(jnp.asarray(split_table(forward_table)), pltpu.HBM),
    )


def planes_kernel(in_ref, forward_ref, inverse_ref, slope_ref, inverse_t_ref, slope_t_ref, out_ref):
    mask = low_lanes((N, 128))
    tiles = [in_ref[:, g].reshape(N, 128) for g in range(4)]
    swapped = [pltpu.roll(tile, DEPTH, 1) for tile in tiles]
    first = [jnp.where(mask, tiles[g], swapped[g + 1]) for g in (0, 2)]
    second = [jnp.where(mask, swapped[g], tiles[g + 1]) for g in (0, 2)]
    stacked = jnp.concatenate(
        [jnp.concatenate(first, axis=1), jnp.concatenate(second, axis=1)], axis=0
    )
    forward = (forward_ref[0], forward_ref[1])
    inverse = (inverse_ref[0], inverse_ref[1])
    slope = (slope_ref[0], slope_ref[1])
    inverse_t = (inverse_t_ref[0], inverse_t_ref[1])
    slope_t = (slope_t_ref[0], slope_t_ref[1])
    depth = dot3(split(stacked), forward, NT)
    step = 2.0 * np.pi / N
    rows = lax.broadcasted_iota(jnp.int32, (N, N), 0)
    columns = lax.broadcasted_iota(jnp.int32, (N, N), 1)
    wave_rows = jnp.where(rows > HALF, rows - HALF, rows).astype(f32) * step
    wave_columns = jnp.where(columns > HALF, columns - HALF, columns).astype(f32) * step
    plane_square = wave_rows * wave_rows + wave_columns * wave_columns
    first_line = lax.axis_index("gy") * lax.axis_size("gz") + lax.axis_index("gz")
    filtered = []
    for part in range(2):
        spectrum = dot3(forward, split(depth[part * N : (part + 1) * N]), NN)
        line = first_line + (HALF if part == 1 else 0) * (first_line == 0).astype(jnp.int32)
        wave_line = line.astype(f32) * step
        square = plane_square + wave_line * wave_line
        filtered.append(
            jnp.where(square > 0.0, spectrum / jnp.where(square > 0.0, square, 1.0), 0.0)
        )
    stacked = split(jnp.concatenate(filtered, axis=0))
    plain = split(dot3(stacked, inverse, NN))
    sloped = split(dot3(stacked, slope, NN))
    part_of = lambda pair, part: tuple(v[part * N : (part + 1) * N] for v in pair)
    for field, (matrix, values) in enumerate(
        ((inverse_t, plain), (slope_t, plain), (inverse_t, sloped))
    ):
        first = dot3(matrix, part_of(values, 0), NN)
        second = dot3(matrix, part_of(values, 1), NN)
        for g in (0, 2):
            lanes = slice(g * DEPTH, g * DEPTH + 128)
            a, b = first[:, lanes], second[:, lanes]
            even = jnp.where(mask, a, pltpu.roll(b, DEPTH, 1))
            odd = jnp.where(mask, pltpu.roll(a, DEPTH, 1), b)
            out_ref[:, g, field * ROWS : (field + 1) * ROWS, :] = even.reshape(32, ROWS, 128)
            out_ref[:, g + 1, field * ROWS : (field + 1) * ROWS, :] = odd.reshape(32, ROWS, 128)


def planes(values, tables):
    whole = pl.BlockSpec(memory_space=pltpu.VMEM)
    return pl.pallas_call(
        planes_kernel,
        in_specs=[whole] * 6,
        out_specs=whole,
        out_shape=jax.ShapeDtypeStruct((32, 4, 3 * ROWS, 128), f32),
        compiler_params=pltpu.CompilerParams(vmem_limit_bytes=24 << 20),
        name="planes",
    )(values, *tables)


PAD = 8
HELD = DEPTH + 2 * PAD
EDGE_ROWS = (0, 1, ROWS - 2, ROWS - 1)


def tile_weights(moved):
    cell = jnp.floor(moved)
    rise = moved - cell
    fall = 1.0 - rise
    rise2, fall2 = rise * rise, fall * fall
    outer_low, outer_high = rise2 * rise, fall2 * fall
    inner_high = 4.0 - 3.0 * (rise2 * (1.0 + fall))
    inner_low = 4.0 - 3.0 * (fall2 * (1.0 + rise))
    pieces = (outer_low, inner_low, inner_high, outer_high)
    at = {n: cell == n for n in range(-4, 4)}
    weights = []
    for offset in range(-2, 3):
        weight = jnp.zeros_like(moved)
        for piece, value in zip(range(-2, 2), pieces):
            weight = jnp.where(at[piece - offset], value, weight)
        weights.append(weight)
    return weights


def row_pair(row, slots, in_ref, displacement_ref, inverse, slope, psi_ref, weight_ref):
    mask = low_lanes((HALF, 128))
    for field in range(3):
        start = field * ROWS + row
        even = in_ref[pl.ds(start, HALF, stride=3 * ROWS), :]
        odd = in_ref[pl.ds(start + 1, HALF, stride=3 * ROWS), :]
        first = jnp.where(mask, even, pltpu.roll(odd, DEPTH, 1))
        second = jnp.where(mask, pltpu.roll(even, DEPTH, 1), odd)
        stacked = jnp.concatenate([first, second], axis=0)
        result = dot3(split(stacked), slope if field == 0 else inverse, TN)
        for part, slot in enumerate(slots):
            values = result[part * DEPTH : (part + 1) * DEPTH]
            psi_ref[slot, field] = values
            for tile in range(DEPTH // 8):
                for half in range(2):
                    lanes = slice(half * 128, half * 128 + 128)
                    rows = slice(tile * 8, tile * 8 + 8)
                    moved = displacement_ref[field, row + part, rows, lanes] + values[rows, lanes]
                    for shift, weight in enumerate(tile_weights(moved)):
                        weight_ref[slot, 5 * field + shift, half, rows, :] = weight


def shift_lines(halves):
    lane = lax.broadcasted_iota(jnp.int32, (8, 128), 1)
    low, high = halves[0][2], halves[1][2]
    for shift_line in (0, 1, 3, 4):
        move = 2 - shift_line
        a = pltpu.roll(halves[0][shift_line], move % 128, 1)
        b = pltpu.roll(halves[1][shift_line], move % 128, 1)
        wraps = lane < move if move > 0 else lane >= 128 + move
        low = low + jnp.where(wraps, b, a)
        high = high + jnp.where(wraps, a, b)
    return low * (1.0 / 216.0), high * (1.0 / 216.0)


def add_up(terms):
    while len(terms) > 1:
        terms = [sum(terms[i : i + 2][1:], terms[i]) for i in range(0, len(terms), 2)]
    return terms[0]


def collect(sum_ref, jobs):
    for half in range(2):
        for shift_depth in range(5):
            for shift_line in range(5):
                zeros = jnp.zeros((PAD, 128), f32)
                sum_ref[half, shift_depth, shift_line, 0:PAD, :] = zeros
                sum_ref[half, shift_depth, shift_line, HELD - PAD : HELD, :] = zeros

    for pairs, out_ref, row in jobs:

        @pl.loop(0, DEPTH // 8)
        def _(tile):
            start = pl.multiple_of(tile * 8, 8)
            for half in range(2):
                totals = None
                for (weight_ref, slot), shift_row in pairs:
                    get = lambda i: weight_ref[slot, i, half, pl.ds(start, 8), :]
                    line_weights = [get(i) for i in range(5)]
                    row_weight = get(5 + shift_row)
                    planes = [row_weight * get(10 + d) for d in range(5)]
                    terms = [[plane * w for w in line_weights] for plane in planes]
                    totals = (
                        terms
                        if totals is None
                        else [[a + b for a, b in zip(x, y)] for x, y in zip(totals, terms)]
                    )
                for d in range(5):
                    for shift_line in range(5):
                        value = totals[d][shift_line]
                        sum_ref[half, d, shift_line, pl.ds(start + PAD, 8), :] = value

        for tile in range(DEPTH // 8 + 1):
            if tile < DEPTH // 8:
                places = [(d, tile * 8 + PAD - 2 + d) for d in range(5)]
            else:
                places = [(d, PAD + DEPTH - 2 + d) for d in (0, 1)]
                places += [(d, d - 2) for d in (3, 4)]
            halves = [
                [
                    add_up([sum_ref[half, d, shift_line, at : at + 8, :] for d, at in places])
                    for shift_line in range(5)
                ]
                for half in range(2)
            ]
            low, high = shift_lines(halves)
            out_ref[row, tile * 8 : tile * 8 + 8, 0:128] = low
            out_ref[row, tile * 8 : tile * 8 + 8, 128:256] = high


def reach(cell, held):
    return [(held[row], row + 2 - cell) for row in sorted(held) if 0 <= row + 2 - cell < 5]


def edges_kernel(
    in_ref, displacement_ref, inverse_ref, slope_ref,
    psi_out, weight_ref, second_ref, first_ref,
    psi_ref, sum_ref, psi_sem,
):
    inverse = (inverse_ref[0], inverse_ref[1])
    slope = (slope_ref[0], slope_ref[1])
    copies = []
    for pair, row in enumerate((0, ROWS - 2)):
        slots = (2 * pair, 2 * pair + 1)
        row_pair(row, slots, in_ref, displacement_ref, inverse, slope, psi_ref, weight_ref)
        for part, slot in enumerate(slots):
            copy = pltpu.make_async_copy(
                psi_ref.at[slot], psi_out.at[:, row + part], psi_sem.at[slot]
            )
            copy.start()
            copies.append(copy)
    held = {row: (weight_ref, slot) for slot, row in enumerate(EDGE_ROWS)}

    def cells(before_ref, after_ref):
        jobs = [(reach(index - 2, held), before_ref, index) for index in range(2)]
        jobs += [(reach(ROWS + index, held), after_ref, index) for index in range(2)]
        collect(sum_ref, jobs)

    odd = lax.axis_index("gy") % 2

    @pl.when(odd == 0)
    def _():
        cells(second_ref, first_ref)

    @pl.when(odd != 0)
    def _():
        cells(first_ref, second_ref)

    for copy in copies:
        copy.wait()


VMEM = pl.BlockSpec(memory_space=pltpu.VMEM)
SMEM = pl.BlockSpec(memory_space=pltpu.SMEM)
ANY = pl.BlockSpec(memory_space=pl.ANY)


def edges(values, displacement, tables):
    halo = jax.ShapeDtypeStruct((2, DEPTH + PAD, N), f32)
    return pl.pallas_call(
        edges_kernel,
        in_specs=[VMEM] * 4,
        out_specs=[ANY, VMEM, VMEM, VMEM],
        out_shape=[
            jax.ShapeDtypeStruct((3, ROWS, DEPTH, N), f32),
            jax.ShapeDtypeStruct((4, 15, 2, DEPTH + PAD, 128), f32),
            halo,
            halo,
        ],
        scratch_shapes=[
            pltpu.VMEM((4, 3, DEPTH, N), f32),
            pltpu.VMEM((2, 5, 5, HELD + PAD, 128), f32),
            pltpu.SemaphoreType.DMA((4,)),
        ],
        compiler_params=pltpu.CompilerParams(vmem_limit_bytes=16 << 20),
        name="edges",
    )(values, displacement, *tables)


def inner_kernel(
    in_ref, displacement_ref, inverse_ref, slope_ref, psi_in, edge_ref,
    psi_out, out_ref,
    psi_ref, weight_ref, sum_ref, psi_sem,
):
    inverse = (inverse_ref[0], inverse_ref[1])
    slope = (slope_ref[0], slope_ref[1])
    copies = []
    for row in (2, 4):
        slots = (row - 2, row - 1)
        row_pair(row, slots, in_ref, displacement_ref, inverse, slope, psi_ref, weight_ref)
        for slot in slots:
            copy = pltpu.make_async_copy(
                psi_ref.at[slot], psi_out.at[:, slot + 2], psi_sem.at[slot]
            )
            copy.start()
            copies.append(copy)
    held = {row: (edge_ref, slot) for slot, row in enumerate(EDGE_ROWS)}
    held.update({row: (weight_ref, row - 2) for row in range(2, ROWS - 2)})
    collect(sum_ref, [(reach(row, held), out_ref, row) for row in range(ROWS)])
    for copy in copies:
        copy.wait()


def inner(values, displacement, tables, psi, weights):
    return pl.pallas_call(
        inner_kernel,
        in_specs=[VMEM] * 4 + [ANY, VMEM],
        out_specs=[ANY, VMEM],
        out_shape=[
            jax.ShapeDtypeStruct((3, ROWS, DEPTH, N), f32),
            jax.ShapeDtypeStruct((ROWS, DEPTH + PAD, N), f32),
        ],
        scratch_shapes=[
            pltpu.VMEM((4, 3, DEPTH, N), f32),
            pltpu.VMEM((4, 15, 2, DEPTH + PAD, 128), f32),
            pltpu.VMEM((2, 5, 5, HELD + PAD, 128), f32),
            pltpu.SemaphoreType.DMA((4,)),
        ],
        input_output_aliases={4: 0},
        compiler_params=pltpu.CompilerParams(vmem_limit_bytes=20 << 20),
        name="inner",
    )(values, displacement, *tables, psi, weights)


def ordered(axis, first, second):
    even = lax.axis_index(axis) % 2 == 0
    return jnp.where(even, second, first), jnp.where(even, first, second)


def sides_kernel(cell_ref, first_ref, second_ref, low_ref, high_ref):
    low, high = ordered("gy", first_ref[...], second_ref[...])
    side = cell_ref[...]
    side = jnp.concatenate(
        [side[0:2] + low, side[2 : ROWS - 2], side[ROWS - 2 :] + high], axis=0
    )
    above, below = side[:, 0:2, :], side[:, PAD - 2 :, :]
    even = lax.axis_index("gz") % 2 == 0
    low_ref[...] = jnp.where(even, above, below)
    high_ref[...] = jnp.where(even, below, above)


def sides(cells, first, second):
    last = DEPTH // PAD
    block = lambda rows: pl.BlockSpec((rows, PAD, N), lambda i: (0, last, 0))
    side = jax.ShapeDtypeStruct((ROWS, 2, N), f32)
    return pl.pallas_call(
        sides_kernel,
        grid=(1,),
        in_specs=[block(ROWS), block(2), block(2)],
        out_specs=[pl.BlockSpec((ROWS, 2, N), lambda i: (0, 0, 0))] * 2,
        out_shape=[side, side],
        compiler_params=pltpu.CompilerParams(vmem_limit_bytes=8 << 20),
        name="sides",
    )(cells, first, second)


def sum_kernel(cell_ref, first_ref, second_ref, near_ref, far_ref, out_ref):
    low, high = ordered("gy", first_ref[:, :DEPTH, :], second_ref[:, :DEPTH, :])
    left, right = ordered("gz", near_ref[...], far_ref[...])
    for row in range(ROWS):
        value = cell_ref[row, :DEPTH, :] - 1.0
        if row < 2:
            value = value + low[row]
        if row >= ROWS - 2:
            value = value + high[row - ROWS + 2]
        out_ref[row, 0:2, :] = value[0:2] + left[row]
        out_ref[row, 2:8, :] = value[2:8]
        out_ref[row, 8:56, :] = value[8:56]
        out_ref[row, 56:62, :] = value[56:62]
        out_ref[row, 62:64, :] = value[62:64] + right[row]


def total(*parts):
    return pl.pallas_call(
        sum_kernel,
        in_specs=[VMEM] * 5,
        out_specs=VMEM,
        out_shape=jax.ShapeDtypeStruct((ROWS, DEPTH, N), f32),
        compiler_params=pltpu.CompilerParams(vmem_limit_bytes=8 << 20),
        name="total",
    )(*parts)


def swap(value, axis, rounds):
    size = lax.axis_size(axis)
    return lax.ppermute(
        value, axis, [(i, (i + (1 if i % 2 == rounds else -1)) % size) for i in range(size)]
    )


def local(hessian_one, hessian_two, displacement):
    both = ("gy", "gz")
    tables = [
        jnp.asarray(split_table(t))
        for t in (forward_table, inverse_table, slope_table, inverse_table.T, slope_table.T)
    ]
    spectra = lines(hessian_one, hessian_two)
    spectra = spectra.reshape(HALF, ROWS, 128)
    spectra = lax.all_to_all(spectra, both, split_axis=0, concat_axis=0, tiled=True)
    returned = planes(spectra.reshape(32, 4, ROWS, 128), tables)
    returned = returned.reshape(HALF, 3 * ROWS, 128)
    returned = lax.all_to_all(returned, both, split_axis=0, concat_axis=0, tiled=True)
    returned = returned.reshape(HALF * 3 * ROWS, 128)
    tables = tables[1:3]
    psi, weights, second, first = edges(returned, displacement, tables)
    second = swap(second, "gy", 1)
    first = swap(first, "gy", 0)
    psi, cells = inner(returned, displacement, tables, psi, weights)
    near, far = sides(cells, first, second)
    far = swap(far, "gz", 1)
    near = swap(near, "gz", 0)
    density = total(cells, first, second, near, far)
    return psi, density


def solution(mesh):
    in_specs = (P(None, "gy", "gz", None), P(None, "gy", "gz", None), P(None, "gy", "gz", None))
    out_specs = (P(None, "gy", "gz", None), P("gy", "gz", None))
    return jax.shard_map(
        local, mesh=mesh, in_specs=in_specs, out_specs=out_specs, check_vma=False
    )
```

```python
import functools

import jax
import jax.numpy as jnp
import numpy as np
from jax import lax
from jax.experimental import pallas as pl
from jax.experimental.pallas import tpu as pltpu
from jax.sharding import PartitionSpec as P


N = 256
HALF = N // 2
ROWS = 8
DEPTH = 64
det_weight = -1.0 / 3.0
mixed_weight = 10.0 / 21.0
f32 = jnp.float32
bf16 = jnp.bfloat16


def split_table(table):
    high = table.astype(np.float32).astype(jnp.bfloat16)
    low = (table - high.astype(np.float64)).astype(np.float32).astype(jnp.bfloat16)
    return np.stack([high, low])


def wave_index():
    order = np.arange(N)
    return np.where(order <= HALF, order, order - HALF)


def real_tables():
    order = np.arange(N)
    wave = wave_index()
    is_sin = order > HALF
    angle = 2.0 * np.pi / N * (wave[:, None] * np.arange(N)[None, :] % N)
    cosine, sine = np.cos(angle), np.sin(angle)
    forward = np.where(is_sin[:, None], sine, cosine)
    single = (order == 0) | (order == HALF)
    weight = np.where(single, 1.0, 2.0)[:, None] / N
    inverse = weight * forward
    number = (2.0 * np.pi / N * np.where(single, 0, wave))[:, None]
    slope = weight * number * np.where(is_sin[:, None], cosine, -sine)
    return forward, inverse, slope


forward_table, inverse_table, slope_table = real_tables()


def split(value):
    high = value.astype(bf16)
    return high, (value - high.astype(f32)).astype(bf16)


def dot3(left, right, dims):
    (left_high, left_low), (right_high, right_low) = left, right
    product = functools.partial(
        lax.dot_general, dimension_numbers=(dims, ((), ())), preferred_element_type=f32
    )
    return product(left_high, right_high) + (
        product(left_high, right_low) + product(left_low, right_high)
    )


NN = ((1,), (0,))
NT = ((1,), (1,))
TN = ((0,), (0,))


def low_lanes(shape):
    return lax.broadcasted_iota(jnp.int32, shape, len(shape) - 1) < DEPTH


def source_term(one, two):
    primary = [one[c].astype(f32) for c in range(6)]
    secondary = [two[c].astype(f32) for c in range(6)]
    determinant = (
        primary[0] * (primary[1] * primary[2] - primary[5] * primary[5])
        - primary[3] * (primary[3] * primary[2] - primary[5] * primary[4])
        + primary[4] * (primary[3] * primary[5] - primary[1] * primary[4])
    )
    mixed = 0.5 * (
        secondary[0] * (primary[1] + primary[2])
        + secondary[1] * (primary[0] + primary[2])
        + secondary[2] * (primary[0] + primary[1])
    )
    mixed = mixed - (
        secondary[3] * primary[3] + secondary[4] * primary[4] + secondary[5] * primary[5]
    )
    return det_weight * determinant + mixed_weight * mixed


def lines_kernel(one_in, two_in, table_in, out_ref, one_ref, two_ref, table_ref, sem):
    table_copy = pltpu.make_async_copy(table_in, table_ref, sem.at[ROWS])
    table_copy.start()
    copies = []
    for pair in range(ROWS // 2):
        rows = slice(2 * pair, 2 * pair + 2)
        for index, (source, target) in enumerate(((one_in, one_ref), (two_in, two_ref))):
            copy = pltpu.make_async_copy(
                source.at[:, rows], target.at[:, rows], sem.at[2 * pair + index]
            )
            copy.start()
            copies.append(copy)
    mask = low_lanes((HALF, 128))
    table_copy.wait()
    for pair in range(ROWS // 2):
        copies[2 * pair].wait()
        copies[2 * pair + 1].wait()
        source = jnp.concatenate(
            [
                source_term(
                    [one_ref[c, row] for c in range(6)], [two_ref[c, row] for c in range(6)]
                )
                for row in (2 * pair, 2 * pair + 1)
            ],
            axis=0,
        )
        result = dot3((table_ref[0], table_ref[1]), split(source), NT)
        first, second = result[:HALF], result[HALF:]
        out_ref[pl.ds(2 * pair, HALF, stride=ROWS), :] = jnp.where(
            mask, first, pltpu.roll(second, DEPTH, 1)
        )
        out_ref[pl.ds(2 * pair + 1, HALF, stride=ROWS), :] = jnp.where(
            mask, pltpu.roll(first, DEPTH, 1), second
        )


def lines(one, two):
    far = pl.BlockSpec(memory_space=pltpu.HBM)
    return pl.pallas_call(
        lines_kernel,
        in_specs=[far] * 3,
        out_specs=pl.BlockSpec(memory_space=pltpu.VMEM),
        out_shape=jax.ShapeDtypeStruct((HALF * ROWS, 128), f32),
        scratch_shapes=[
            pltpu.VMEM((6, ROWS, DEPTH, N), bf16),
            pltpu.VMEM((6, ROWS, DEPTH, N), bf16),
            pltpu.VMEM((2, N, N), bf16),
            pltpu.SemaphoreType.DMA((ROWS + 1,)),
        ],
        compiler_params=pltpu.CompilerParams(vmem_limit_bytes=16 << 20),
        name="lines",
    )(
        pltpu.with_memory_space_constraint(one, pltpu.HBM),
        pltpu.with_memory_space_constraint(two, pltpu.HBM),
        pltpu.with_memory_space_constraint(jnp.asarray(split_table(forward_table)), pltpu.HBM),
    )


def planes_kernel(in_ref, forward_ref, inverse_ref, slope_ref, inverse_t_ref, slope_t_ref, out_ref):
    mask = low_lanes((N, 128))
    tiles = [in_ref[:, g].reshape(N, 128) for g in range(4)]
    swapped = [pltpu.roll(tile, DEPTH, 1) for tile in tiles]
    first = [jnp.where(mask, tiles[g], swapped[g + 1]) for g in (0, 2)]
    second = [jnp.where(mask, swapped[g], tiles[g + 1]) for g in (0, 2)]
    stacked = jnp.concatenate(
        [jnp.concatenate(first, axis=1), jnp.concatenate(second, axis=1)], axis=0
    )
    forward = (forward_ref[0], forward_ref[1])
    inverse = (inverse_ref[0], inverse_ref[1])
    slope = (slope_ref[0], slope_ref[1])
    inverse_t = (inverse_t_ref[0], inverse_t_ref[1])
    slope_t = (slope_t_ref[0], slope_t_ref[1])
    depth = dot3(split(stacked), forward, NT)
    step = 2.0 * np.pi / N
    rows = lax.broadcasted_iota(jnp.int32, (N, N), 0)
    columns = lax.broadcasted_iota(jnp.int32, (N, N), 1)
    wave_rows = jnp.where(rows > HALF, rows - HALF, rows).astype(f32) * step
    wave_columns = jnp.where(columns > HALF, columns - HALF, columns).astype(f32) * step
    plane_square = wave_rows * wave_rows + wave_columns * wave_columns
    first_line = lax.axis_index("gy") * lax.axis_size("gz") + lax.axis_index("gz")
    filtered = []
    for part in range(2):
        spectrum = dot3(forward, split(depth[part * N : (part + 1) * N]), NN)
        line = first_line + (HALF if part == 1 else 0) * (first_line == 0).astype(jnp.int32)
        wave_line = line.astype(f32) * step
        square = plane_square + wave_line * wave_line
        filtered.append(
            jnp.where(square > 0.0, spectrum / jnp.where(square > 0.0, square, 1.0), 0.0)
        )
    stacked = split(jnp.concatenate(filtered, axis=0))
    plain = split(dot3(stacked, inverse, NN))
    sloped = split(dot3(stacked, slope, NN))
    part_of = lambda pair, part: tuple(v[part * N : (part + 1) * N] for v in pair)
    for field, (matrix, values) in enumerate(
        ((inverse_t, plain), (slope_t, plain), (inverse_t, sloped))
    ):
        first = dot3(matrix, part_of(values, 0), NN)
        second = dot3(matrix, part_of(values, 1), NN)
        for g in (0, 2):
            lanes = slice(g * DEPTH, g * DEPTH + 128)
            a, b = first[:, lanes], second[:, lanes]
            even = jnp.where(mask, a, pltpu.roll(b, DEPTH, 1))
            odd = jnp.where(mask, pltpu.roll(a, DEPTH, 1), b)
            out_ref[:, g, field * ROWS : (field + 1) * ROWS, :] = even.reshape(32, ROWS, 128)
            out_ref[:, g + 1, field * ROWS : (field + 1) * ROWS, :] = odd.reshape(32, ROWS, 128)


def planes(values, tables):
    whole = pl.BlockSpec(memory_space=pltpu.VMEM)
    return pl.pallas_call(
        planes_kernel,
        in_specs=[whole] * 6,
        out_specs=whole,
        out_shape=jax.ShapeDtypeStruct((32, 4, 3 * ROWS, 128), f32),
        compiler_params=pltpu.CompilerParams(vmem_limit_bytes=24 << 20),
        name="planes",
    )(values, *tables)


PAD = 8
HELD = DEPTH + 2 * PAD


def tile_weights(moved):
    cell = jnp.floor(moved)
    rise = moved - cell
    fall = 1.0 - rise
    rise2, fall2 = rise * rise, fall * fall
    outer_low, outer_high = rise2 * rise, fall2 * fall
    inner_high = 4.0 - 3.0 * (rise2 * (1.0 + fall))
    inner_low = 4.0 - 3.0 * (fall2 * (1.0 + rise))
    pieces = (outer_low, inner_low, inner_high, outer_high)
    at = {n: cell == n for n in range(-4, 4)}
    weights = []
    for offset in range(-2, 3):
        weight = jnp.zeros_like(moved)
        for piece, value in zip(range(-2, 2), pieces):
            weight = jnp.where(at[piece - offset], value, weight)
        weights.append(weight)
    return weights


def row_pair(row, slots, in_ref, displacement_ref, inverse, slope, psi_ref, weight_ref):
    mask = low_lanes((HALF, 128))
    for field in range(3):
        start = field * ROWS + row
        even = in_ref[pl.ds(start, HALF, stride=3 * ROWS), :]
        odd = in_ref[pl.ds(start + 1, HALF, stride=3 * ROWS), :]
        first = jnp.where(mask, even, pltpu.roll(odd, DEPTH, 1))
        second = jnp.where(mask, pltpu.roll(even, DEPTH, 1), odd)
        stacked = jnp.concatenate([first, second], axis=0)
        result = dot3(split(stacked), slope if field == 0 else inverse, TN)
        for part, slot in enumerate(slots):
            values = result[part * DEPTH : (part + 1) * DEPTH]
            psi_ref[slot, field] = values
            for tile in range(DEPTH // 8):
                for half in range(2):
                    lanes = slice(half * 128, half * 128 + 128)
                    rows = slice(tile * 8, tile * 8 + 8)
                    moved = displacement_ref[field, row + part, rows, lanes] + values[rows, lanes]
                    for shift, weight in enumerate(tile_weights(moved)):
                        weight_ref[slot, 5 * field + shift, half, rows, :] = weight


def shift_lines(halves):
    lane = lax.broadcasted_iota(jnp.int32, (8, 128), 1)
    low, high = halves[0][2], halves[1][2]
    for shift_line in (0, 1, 3, 4):
        move = 2 - shift_line
        a = pltpu.roll(halves[0][shift_line], move % 128, 1)
        b = pltpu.roll(halves[1][shift_line], move % 128, 1)
        wraps = lane < move if move > 0 else lane >= 128 + move
        low = low + jnp.where(wraps, b, a)
        high = high + jnp.where(wraps, a, b)
    return low * (1.0 / 216.0), high * (1.0 / 216.0)


def add_up(terms):
    while len(terms) > 1:
        terms = [sum(terms[i : i + 2][1:], terms[i]) for i in range(0, len(terms), 2)]
    return terms[0]


def collect(sum_ref, jobs):
    for half in range(2):
        for shift_depth in range(5):
            for shift_line in range(5):
                zeros = jnp.zeros((PAD, 128), f32)
                sum_ref[half, shift_depth, shift_line, 0:PAD, :] = zeros
                sum_ref[half, shift_depth, shift_line, HELD - PAD : HELD, :] = zeros

    for pairs, out_ref, row in jobs:

        @pl.loop(0, DEPTH // 8)
        def _(tile):
            start = pl.multiple_of(tile * 8, 8)
            for half in range(2):
                totals = None
                for (weight_ref, slot), shift_row in pairs:
                    get = lambda i: weight_ref[slot, i, half, pl.ds(start, 8), :]
                    line_weights = [get(i) for i in range(5)]
                    row_weight = get(5 + shift_row)
                    planes = [row_weight * get(10 + d) for d in range(5)]
                    terms = [[plane * w for w in line_weights] for plane in planes]
                    totals = (
                        terms
                        if totals is None
                        else [[a + b for a, b in zip(x, y)] for x, y in zip(totals, terms)]
                    )
                for d in range(5):
                    for shift_line in range(5):
                        value = totals[d][shift_line]
                        sum_ref[half, d, shift_line, pl.ds(start + PAD, 8), :] = value

        for tile in range(DEPTH // 8 + 1):
            if tile < DEPTH // 8:
                places = [(d, tile * 8 + PAD - 2 + d) for d in range(5)]
            else:
                places = [(d, PAD + DEPTH - 2 + d) for d in (0, 1)]
                places += [(d, d - 2) for d in (3, 4)]
            halves = [
                [
                    add_up([sum_ref[half, d, shift_line, at : at + 8, :] for d, at in places])
                    for shift_line in range(5)
                ]
                for half in range(2)
            ]
            low, high = shift_lines(halves)
            out_ref[row, tile * 8 : tile * 8 + 8, 0:128] = low
            out_ref[row, tile * 8 : tile * 8 + 8, 128:256] = high


def reach(cell, held):
    return [(held[row], row + 2 - cell) for row in sorted(held) if 0 <= row + 2 - cell < 5]


VMEM = pl.BlockSpec(memory_space=pltpu.VMEM)
ANY = pl.BlockSpec(memory_space=pl.ANY)


def edge_kernel(
    far, in_ref, displacement_ref, inverse_ref, slope_ref, *refs,
):
    psi_out, weight_ref, halo_ref, psi_ref, sum_ref, psi_sem = refs[-6:]
    inverse = (inverse_ref[0], inverse_ref[1])
    slope = (slope_ref[0], slope_ref[1])
    even = lax.axis_index("gy") % 2 == 0
    low = even if far else jnp.logical_not(even)
    row = jnp.where(low, 0, ROWS - 2)
    row_pair(row, (0, 1), in_ref, displacement_ref, inverse, slope, psi_ref, weight_ref)
    copies = []
    for slot in range(2):
        copy = pltpu.make_async_copy(psi_ref.at[slot], psi_out.at[:, row + slot], psi_sem.at[slot])
        copy.start()
        copies.append(copy)

    @pl.when(low)
    def _():
        held = {0: (weight_ref, 0), 1: (weight_ref, 1)}
        collect(sum_ref, [(reach(index - 2, held), halo_ref, index) for index in range(2)])

    @pl.when(jnp.logical_not(low))
    def _():
        held = {ROWS - 2: (weight_ref, 0), ROWS - 1: (weight_ref, 1)}
        collect(sum_ref, [(reach(ROWS + index, held), halo_ref, index) for index in range(2)])

    for copy in copies:
        copy.wait()


def edge(far, values, displacement, tables, *psi):
    return pl.pallas_call(
        functools.partial(edge_kernel, far),
        in_specs=[VMEM] * 4 + [ANY] * len(psi),
        out_specs=[ANY, VMEM, VMEM],
        out_shape=[
            jax.ShapeDtypeStruct((3, ROWS, DEPTH, N), f32),
            jax.ShapeDtypeStruct((2, 15, 2, DEPTH + PAD, 128), f32),
            jax.ShapeDtypeStruct((2, DEPTH + PAD, N), f32),
        ],
        scratch_shapes=[
            pltpu.VMEM((2, 3, DEPTH, N), f32),
            pltpu.VMEM((2, 5, 5, HELD + PAD, 128), f32),
            pltpu.SemaphoreType.DMA((2,)),
        ],
        input_output_aliases={4: 0} if psi else {},
        compiler_params=pltpu.CompilerParams(vmem_limit_bytes=16 << 20),
        name="far_edge" if far else "near_edge",
    )(values, displacement, *tables, *psi)


def inner_kernel(
    in_ref, displacement_ref, inverse_ref, slope_ref, psi_in, far_ref, near_ref,
    psi_out, out_ref,
    psi_ref, weight_ref, sum_ref, psi_sem,
):
    inverse = (inverse_ref[0], inverse_ref[1])
    slope = (slope_ref[0], slope_ref[1])
    copies = []
    for row in (2, 4):
        slots = (row - 2, row - 1)
        row_pair(row, slots, in_ref, displacement_ref, inverse, slope, psi_ref, weight_ref)
        for slot in slots:
            copy = pltpu.make_async_copy(
                psi_ref.at[slot], psi_out.at[:, slot + 2], psi_sem.at[slot]
            )
            copy.start()
            copies.append(copy)

    def cells(low_ref, high_ref):
        held = {row: (weight_ref, row - 2) for row in range(2, ROWS - 2)}
        for slot in range(2):
            held[slot] = (low_ref, slot)
            held[ROWS - 2 + slot] = (high_ref, slot)
        collect(sum_ref, [(reach(row, held), out_ref, row) for row in range(ROWS)])

    even = lax.axis_index("gy") % 2 == 0

    @pl.when(even)
    def _():
        cells(far_ref, near_ref)

    @pl.when(jnp.logical_not(even))
    def _():
        cells(near_ref, far_ref)

    for copy in copies:
        copy.wait()


def inner(values, displacement, tables, psi, far, near):
    return pl.pallas_call(
        inner_kernel,
        in_specs=[VMEM] * 4 + [ANY, VMEM, VMEM],
        out_specs=[ANY, VMEM],
        out_shape=[
            jax.ShapeDtypeStruct((3, ROWS, DEPTH, N), f32),
            jax.ShapeDtypeStruct((ROWS, DEPTH + PAD, N), f32),
        ],
        scratch_shapes=[
            pltpu.VMEM((4, 3, DEPTH, N), f32),
            pltpu.VMEM((4, 15, 2, DEPTH + PAD, 128), f32),
            pltpu.VMEM((2, 5, 5, HELD + PAD, 128), f32),
            pltpu.SemaphoreType.DMA((4,)),
        ],
        input_output_aliases={4: 0},
        compiler_params=pltpu.CompilerParams(vmem_limit_bytes=20 << 20),
        name="inner",
    )(values, displacement, *tables, psi, far, near)


def ordered(axis, first, second):
    even = lax.axis_index(axis) % 2 == 0
    return jnp.where(even, second, first), jnp.where(even, first, second)


def sides_kernel(cell_ref, first_ref, second_ref, low_ref, high_ref):
    low, high = ordered("gy", first_ref[...], second_ref[...])
    side = cell_ref[...]
    side = jnp.concatenate(
        [side[0:2] + low, side[2 : ROWS - 2], side[ROWS - 2 :] + high], axis=0
    )
    above, below = side[:, 0:2, :], side[:, PAD - 2 :, :]
    even = lax.axis_index("gz") % 2 == 0
    low_ref[...] = jnp.where(even, above, below)
    high_ref[...] = jnp.where(even, below, above)


def sides(cells, first, second):
    last = DEPTH // PAD
    block = lambda rows: pl.BlockSpec((rows, PAD, N), lambda i: (0, last, 0))
    side = jax.ShapeDtypeStruct((ROWS, 2, N), f32)
    return pl.pallas_call(
        sides_kernel,
        grid=(1,),
        in_specs=[block(ROWS), block(2), block(2)],
        out_specs=[pl.BlockSpec((ROWS, 2, N), lambda i: (0, 0, 0))] * 2,
        out_shape=[side, side],
        compiler_params=pltpu.CompilerParams(vmem_limit_bytes=8 << 20),
        name="sides",
    )(cells, first, second)


def sum_kernel(cell_ref, first_ref, second_ref, near_ref, far_ref, out_ref):
    low, high = ordered("gy", first_ref[:, :DEPTH, :], second_ref[:, :DEPTH, :])
    left, right = ordered("gz", near_ref[...], far_ref[...])
    for row in range(ROWS):
        value = cell_ref[row, :DEPTH, :] - 1.0
        if row < 2:
            value = value + low[row]
        if row >= ROWS - 2:
            value = value + high[row - ROWS + 2]
        out_ref[row, 0:2, :] = value[0:2] + left[row]
        out_ref[row, 2:8, :] = value[2:8]
        out_ref[row, 8:56, :] = value[8:56]
        out_ref[row, 56:62, :] = value[56:62]
        out_ref[row, 62:64, :] = value[62:64] + right[row]


def total(*parts):
    return pl.pallas_call(
        sum_kernel,
        in_specs=[VMEM] * 5,
        out_specs=VMEM,
        out_shape=jax.ShapeDtypeStruct((ROWS, DEPTH, N), f32),
        compiler_params=pltpu.CompilerParams(vmem_limit_bytes=8 << 20),
        name="total",
    )(*parts)


def swap(value, axis, rounds):
    size = lax.axis_size(axis)
    return lax.ppermute(
        value, axis, [(i, (i + (1 if i % 2 == rounds else -1)) % size) for i in range(size)]
    )


def local(hessian_one, hessian_two, displacement):
    both = ("gy", "gz")
    tables = [
        jnp.asarray(split_table(t))
        for t in (forward_table, inverse_table, slope_table, inverse_table.T, slope_table.T)
    ]
    spectra = lines(hessian_one, hessian_two)
    spectra = spectra.reshape(HALF, ROWS, 128)
    spectra = lax.all_to_all(spectra, both, split_axis=0, concat_axis=0, tiled=True)
    returned = planes(spectra.reshape(32, 4, ROWS, 128), tables)
    returned = returned.reshape(HALF, 3 * ROWS, 128)
    returned = lax.all_to_all(returned, both, split_axis=0, concat_axis=0, tiled=True)
    returned = returned.reshape(HALF * 3 * ROWS, 128)
    tables = tables[1:3]
    psi, far_weights, second = edge(True, returned, displacement, tables)
    second = swap(second, "gy", 1)
    psi, near_weights, first = edge(False, returned, displacement, tables, psi)
    first = swap(first, "gy", 0)
    psi, cells = inner(returned, displacement, tables, psi, far_weights, near_weights)
    near, far = sides(cells, first, second)
    far = swap(far, "gz", 1)
    near = swap(near, "gz", 0)
    density = total(cells, first, second, near, far)
    return psi, density


def solution(mesh):
    in_specs = (P(None, "gy", "gz", None), P(None, "gy", "gz", None), P(None, "gy", "gz", None))
    out_specs = (P(None, "gy", "gz", None), P("gy", "gz", None))
    return jax.shard_map(
        local, mesh=mesh, in_specs=in_specs, out_specs=out_specs, check_vma=False
    )
```
